32 devices in a mesh: patch: 8 (over z, x), lev: 4 (over y, core).
Axes of the slice: x: 2, y: 2, z: 4, core: 2. Of those that a mesh axis runs over, the one named last changes fastest.
Arguments:
- tracer_field: float32 [80, 3, 16384], P('lev', None, 'patch'), may hold values from -6 to 6
- send_coarse1: int32 [8, 2, 128], P('patch'), may hold values from 0 to 1023
- send_detail1: int32 [8, 2, 128], P('patch'), may hold values from 0 to 1023
- send_coarse2: int32 [8, 2, 64], P('patch'), may hold values from 0 to 511
- send_detail2: int32 [8, 2, 64], P('patch'), may hold values from 0 to 511
- predict_links1: int32 [8, 8192], P(None, 'patch'), may hold values from 0 to 1279
- predict_weights1: float32 [8, 8192], P(None, 'patch'), may hold values from 0.02 to 0.22
- update_links1: int32 [8, 8192], P(None, 'patch'), may hold values from 0 to 1279
- update_weights1: float32 [8, 8192], P(None, 'patch'), may hold values from 0.02 to 0.14
- predict_links2: int32 [8, 4096], P(None, 'patch'), may hold values from 0 to 639
- predict_weights2: float32 [8, 4096], P(None, 'patch'), may hold values from 0.02 to 0.22
- update_links2: int32 [8, 4096], P(None, 'patch'), may hold values from 0 to 639
- update_weights2: float32 [8, 4096], P(None, 'patch'), may hold values from 0.02 to 0.14
Outputs:
- coefficients: float32 [80, 3, 16384], P(None, None, ('patch', 'lev'))
The draws below stay inside these ranges and needn't reach their ends.
Inputs may be any that keep to these rules, and one draw needn't show every extreme that they name: `send_coarse1`: row lists index a patch's own coarse or detail rows of that level. `predict_links1`: links index the patch's own rows first, then the 128 rows from the left neighbour, then the 128 from the right. `predict_links2`: links index the patch's own rows first, then the 64 rows from the left neighbour, then the 64 from the right.
All inputs are finite; a program needn't handle non-finite values.
Results may differ from the reference program's by a relative error of at most 0.00007.
Values sent between devices are 32-bit elements; how exact they have to be, the bound alone decides.
A program may use at most 64 MiB of HBM per device.

```python
import jax
import jax.numpy as jnp
from jax import lax

LEVELS = 80
TRACERS = 3
NBRS = 8
CELL_DEV = 2048
PATCHES = 8
CELLS = 16384
HALO1 = 128
HALO2 = 64


def touch_ends(entries, own_key, smallest, high):
    longest = entries.shape.index(max(entries.shape))
    spots = []
    for shift in (0, 1):
        where = [jax.random.randint(jax.random.fold_in(own_key, axis), (), 0, length) for axis, length in enumerate(entries.shape)]
        where[longest] = (where[longest] + shift) % entries.shape[longest]
        spots.append(tuple(where))
    return entries.at[spots[0]].set(smallest).at[spots[1]].set(high)


def shard_levels(key, shape, cuts, least, top_value):
    loudness = 1.0
    for axis_at, shards_of in cuts:
        heights = jax.random.uniform(jax.random.fold_in(jax.random.fold_in(key, 6), axis_at), (shards_of,), jnp.float32, least / len(cuts), top_value / len(cuts))
        loudness = loudness * jnp.repeat(jnp.exp(heights), shape[axis_at] // shards_of).reshape((-1,) + (1,) * (len(shape) - 1 - axis_at))
    return loudness


def centred(own_key, extent, scale, bound, split=(), held_as=jnp.bfloat16):
    drawn = jax.random.normal(own_key, extent, jnp.float32) * scale
    if len(split) > 0:
        drawn = shard_levels(own_key, extent, split, -0.22, 0.18) * drawn
    return jnp.clip(drawn, min=-bound, max=bound).astype(held_as)


def setup_inputs(seed: int = 0) -> dict:
    splits = jax.random.split(jax.random.key(seed), 14)
    return {
        "tracer_field": centred(splits[0], (LEVELS, TRACERS, CELLS), 1.0, 6.0, ((0, 4), (2, 8)), jnp.float32),
        "send_coarse1": touch_ends(jax.random.randint(splits[1], (PATCHES, 2, HALO1), 0, CELL_DEV // 2), jax.random.fold_in(splits[1], 1), 0, (CELL_DEV // 2) - 1).astype(jnp.int32),
        "send_detail1": touch_ends(jax.random.randint(splits[2], (PATCHES, 2, HALO1), 0, CELL_DEV // 2), jax.random.fold_in(splits[2], 1), 0, (CELL_DEV // 2) - 1).astype(jnp.int32),
        "send_coarse2": touch_ends(jax.random.randint(splits[3], (PATCHES, 2, HALO2), 0, CELL_DEV // 4), jax.random.fold_in(splits[3], 1), 0, (CELL_DEV // 4) - 1).astype(jnp.int32),
        "send_detail2": touch_ends(jax.random.randint(splits[4], (PATCHES, 2, HALO2), 0, CELL_DEV // 4), jax.random.fold_in(splits[4], 1), 0, (CELL_DEV // 4) - 1).astype(jnp.int32),
        "predict_links1": touch_ends(jax.random.randint(splits[5], (NBRS, CELLS // 2), 0, CELL_DEV // 2 + CELL_DEV // 8), jax.random.fold_in(splits[5], 1), 0, (CELL_DEV // 2 + CELL_DEV // 8) - 1).astype(jnp.int32),
        "predict_weights1": jnp.clip(0.02 + 0.2 * jax.random.uniform(splits[6], (NBRS, CELLS // 2), jnp.float32) ** shard_levels(splits[6], (NBRS, CELLS // 2), ((1, 8),), -0.2, 0.2), 0.02, 0.22),
        "update_links1": touch_ends(jax.random.randint(splits[7], (NBRS, CELLS // 2), 0, CELL_DEV // 2 + CELL_DEV // 8), jax.random.fold_in(splits[7], 1), 0, (CELL_DEV // 2 + CELL_DEV // 8) - 1).astype(jnp.int32),
        "update_weights1": jnp.clip(0.02 + 0.12000000104308128 * jax.random.uniform(splits[8], (NBRS, CELLS // 2), jnp.float32) ** shard_levels(splits[8], (NBRS, CELLS // 2), ((1, 8),), -0.2, 0.2), 0.02, 0.14),
        "predict_links2": touch_ends(jax.random.randint(splits[9], (NBRS, CELLS // 4), 0, CELL_DEV // 4 + CELL_DEV // 16), jax.random.fold_in(splits[9], 1), 0, (CELL_DEV // 4 + CELL_DEV // 16) - 1).astype(jnp.int32),
        "predict_weights2": jnp.clip(0.02 + 0.2 * jax.random.uniform(splits[10], (NBRS, CELLS // 4), jnp.float32) ** shard_levels(splits[10], (NBRS, CELLS // 4), ((1, 8),), -0.2, 0.2), 0.02, 0.22),
        "update_links2": touch_ends(jax.random.randint(splits[11], (NBRS, CELLS // 4), 0, CELL_DEV // 4 + CELL_DEV // 16), jax.random.fold_in(splits[11], 1), 0, (CELL_DEV // 4 + CELL_DEV // 16) - 1).astype(jnp.int32),
        "update_weights2": jnp.clip(0.02 + 0.12000000104308128 * jax.random.uniform(splits[12], (NBRS, CELLS // 4), jnp.float32) ** shard_levels(splits[12], (NBRS, CELLS // 4), ((1, 8),), -0.2, 0.2), 0.02, 0.14),
    }


def cosine_table(length):
    rows = jnp.arange(length).astype(jnp.float32)[:, None]
    columns = jnp.arange(length).astype(jnp.float32)[None, :]
    matrix = jnp.cos(jnp.pi * (columns + 0.5) * rows / length) * jnp.sqrt(2.0 / length)
    first = jnp.where(rows == 0.0, jnp.sqrt(0.5), 1.0)
    return (matrix * first).astype(jnp.float32)

def extend(values, send_rows):
    patch_index = jnp.arange(values.shape[2])[:, None]
    first = values[:, :, patch_index, send_rows[:, 0, :]]
    second = values[:, :, patch_index, send_rows[:, 1, :]]
    from_left = jnp.roll(second, 1, axis=2)
    from_right = jnp.roll(first, -1, axis=2)
    return jnp.concatenate([values, from_left, from_right], axis=3)

def weighted(extended, links, weights):
    patch_index = jnp.arange(extended.shape[2])[:, None]
    total = jnp.zeros(extended.shape[:3] + (links.shape[2],), jnp.float32)
    for neighbour in range(links.shape[0]):
        total = total + weights[neighbour] * extended[:, :, patch_index, links[neighbour]]
    return total

def lift(values, send_coarse, send_detail, predict_links, predict_weights, update_links, update_weights):
    patches = values.shape[2]
    half_cells = values.shape[3] // 2
    fine_part = values[..., :half_cells]
    coarse = values[..., half_cells:]
    plinks = predict_links.reshape(predict_links.shape[0], patches, half_cells)
    pweights = predict_weights.reshape(predict_weights.shape[0], patches, half_cells)
    ulinks = update_links.reshape(update_links.shape[0], patches, half_cells)
    uweights = update_weights.reshape(update_weights.shape[0], patches, half_cells)
    detail = fine_part - weighted(extend(coarse, send_coarse), plinks, pweights)
    smooth = coarse + weighted(extend(detail, send_detail), ulinks, uweights)
    return (detail, smooth)

def reference(tracer_field, send_coarse1, send_detail1, send_coarse2, send_detail2, predict_links1, predict_weights1, update_links1, update_weights1, predict_links2, predict_weights2, update_links2, update_weights2):
    values = tracer_field.reshape(LEVELS, TRACERS, PATCHES, CELL_DEV)
    detail1, smooth1 = lift(values, send_coarse1, send_detail1, predict_links1, predict_weights1, update_links1, update_weights1)
    detail2, smooth2 = lift(smooth1, send_coarse2, send_detail2, predict_links2, predict_weights2, update_links2, update_weights2)
    bands = jnp.concatenate([detail1, detail2, smooth2], axis=3).reshape(LEVELS, TRACERS, CELLS)
    table = cosine_table(LEVELS)
    return jnp.einsum('km,mtc->ktc', table, bands, precision=lax.Precision.HIGHEST)
```

```python
import functools

import jax
import jax.numpy as jnp
import ml_dtypes
import numpy as np
from jax import lax
from jax.experimental import pallas as pl
from jax.experimental.pallas import tpu as pltpu
from jax.sharding import PartitionSpec as P

LANES = 128
SUB = 8
MESH = pl.DeviceIdType.MESH


def cosine_table(length):
    rows = np.arange(length, dtype=np.float64)[:, None]
    columns = np.arange(length, dtype=np.float64)[None, :]
    matrix = np.cos(np.pi * (columns + 0.5) * rows / length) * np.sqrt(2.0 / length)
    matrix[0] *= np.sqrt(0.5)
    return matrix


def spread_table(levels, tracers, groups, padded):
    own = levels // groups
    table = cosine_table(levels).reshape(levels, groups, own)
    wide = np.zeros((tracers, levels, groups, padded))
    for t in range(tracers):
        wide[t, :, :, t * own : (t + 1) * own] = table
    wide = wide.reshape(levels * tracers, groups * padded).astype(np.float32)
    high = wide.astype(ml_dtypes.bfloat16)
    low = (wide - high.astype(np.float32)).astype(ml_dtypes.bfloat16)
    return high, low


def halves(x):
    high = x.astype(jnp.bfloat16)
    low = (x - high.astype(jnp.float32)).astype(jnp.bfloat16)
    return high, low


def along(table, index):
    numbers = lax.GatherDimensionNumbers(
        offset_dims=(),
        collapsed_slice_dims=(0,),
        start_index_map=(0,),
        operand_batching_dims=(1,),
        start_indices_batching_dims=(1,),
    )
    mode = lax.GatherScatterMode.PROMISE_IN_BOUNDS
    return lax.gather(table, index[:, :, None], numbers, (1, 1), mode=mode)


def tile(links, weights, merged, cols, blocks):
    slots = links.shape[0]
    lane = []
    block = []
    weight = []
    for k in range(slots):
        link = jnp.broadcast_to(links[k : k + 1, cols], (SUB, LANES))
        lane.append(link & (LANES - 1))
        block.append(link >> 7)
        weight.append(jnp.broadcast_to(weights[k : k + 1, cols], (SUB, LANES)))
    which = lax.broadcasted_iota(jnp.int32, (SUB, LANES), 0)
    same = [[lane[j] == lane[k] for j in range(k)] for k in range(slots)]
    for g in range(-(-blocks // SUB)):
        placed = []
        for k in range(slots):
            mine = jnp.where(block[k] == which + g * SUB, weight[k], 0.0)
            total = mine
            for j in range(k):
                total = total + jnp.where(same[k][j], placed[j], 0.0)
            placed.append(mine)
            merged[k, g * SUB : (g + 1) * SUB, :] = total
    none = jnp.zeros((2 * SUB - slots, LANES), jnp.float32)
    tables = [halves(jnp.concatenate([merged[:, b, :], none], axis=0)) for b in range(blocks)]
    short = [jnp.concatenate([v, v], axis=0).astype(jnp.int16) for v in lane]
    strips = []
    for s in range(LANES // (2 * SUB)):
        rows = lax.broadcasted_iota(jnp.int16, (2 * SUB, LANES), 0) + jnp.int16(s * 2 * SUB)
        index = jnp.full((2 * SUB, LANES), slots, jnp.int16)
        for k in range(slots):
            index = jnp.where(short[k] == rows, jnp.int16(k), index)
        strips.append(index)
    return tables, strips


def spread(tiles, part, first, last):
    return jnp.concatenate(
        [
            jnp.concatenate(
                [along(tables[b][part], index) for b in range(first, last) for index in strips],
                axis=0,
            )
            for tables, strips in tiles
        ],
        axis=1,
    )


def stage(links, weights, merged, first, count, own, blocks, ext, tail_high, tail_low, emit):
    padded = ext.shape[0] // 2
    depth = own * LANES

    def step(t, _):
        start = pl.multiple_of(first + t * 2 * LANES, 2 * LANES)
        tiles = [
            tile(
                links, weights, merged.at[h],
                pl.ds(pl.multiple_of(start + h * LANES, LANES), LANES), blocks,
            )
            for h in range(2)
        ]
        high = spread(tiles, 0, 0, own)
        low = spread(tiles, 1, 0, own)
        both = jnp.dot(ext[:, 0:depth], high, preferred_element_type=jnp.float32)
        rest = jnp.dot(ext[0:padded, 0:depth], low, preferred_element_type=jnp.float32)
        cols = pl.ds(start, 2 * LANES)
        emit(cols, both[0:padded] + both[padded : 2 * padded] + rest)
        tail_high[:, cols] = spread(tiles, 0, own, blocks)
        tail_low[:, cols] = spread(tiles, 1, own, blocks)
        return 0

    lax.fori_loop(0, count // (2 * LANES), step, 0)


def picked(source, start, blocks, index, out):
    lane = jnp.broadcast_to(index & (LANES - 1), (SUB, LANES))
    block = jnp.broadcast_to(index >> 7, (SUB, LANES))
    for r in range(source.shape[0] // SUB):
        rows = slice(r * SUB, (r + 1) * SUB)
        got = None
        for b in range(blocks):
            cols = slice(start + b * LANES, start + (b + 1) * LANES)
            t = jnp.take_along_axis(source[rows, cols], lane, axis=1)
            got = t if got is None else jnp.where(block == b, t, got)
        out[rows, :] = got


def put(ext, padded, at, value):
    high, low = halves(value)
    width = value.shape[1]
    ext[0:padded, at : at + width] = high
    ext[padded : 2 * padded, at : at + width] = low


def product(ext, padded, start, w_high, w_low, cols):
    k = slice(start, start + w_high.shape[0])
    both = jnp.dot(ext[:, k], w_high[:, cols], preferred_element_type=jnp.float32)
    rest = jnp.dot(ext[0:padded, k], w_low[:, cols], preferred_element_type=jnp.float32)
    return both[0:padded] + both[padded : 2 * padded] + rest


def reach(value, links, weights, start, width):
    padded = value.shape[0]
    rows = [value[r * SUB : (r + 1) * SUB, :] for r in range(padded // SUB)]
    totals = [None] * len(rows)
    for k in range(links.shape[0]):
        link = jnp.broadcast_to(links[k : k + 1, :], (SUB, LANES))
        weight = jnp.broadcast_to(weights[k : k + 1, :], (SUB, LANES))
        weight = jnp.where((link >= start) & (link < start + width), weight, 0.0)
        lane = link & (LANES - 1)
        for r, row in enumerate(rows):
            term = weight * jnp.take_along_axis(row, lane, axis=1)
            totals[r] = term if totals[r] is None else totals[r] + term
    return jnp.concatenate(totals, axis=0)


def body(
    n_patch, n_lev, levels,
    field, sc1, sd1, sc2, sd2, pl1, pw1, ul1, uw1, pl2, pw2, ul2, uw2,
    gathered,
    xs, ext, merged, t1h, t1l, t2h, t2l,
    det1, sm1, det2, sm2, hsend, hrecv,
    ext2, glink, gweight, rlink, rweight, part, full1, full2, done, early,
    ms_sem, mr_sem,
    hs_sem, hr_sem, as_sem, ar_sem,
):
    tracers, own, cells = field.shape
    rows = own * tracers
    padded = xs.shape[0]
    n1 = cells // 2
    n2 = cells // 4
    halo1 = sc1.shape[2]
    halo2 = sc2.shape[2]
    chunk = cells // n_lev
    me = lax.axis_index("lev")
    patch = lax.axis_index("patch")
    left = lax.rem(patch + n_patch - 1, n_patch)
    right = lax.rem(patch + 1, n_patch)

    barrier = pltpu.get_barrier_semaphore()
    for neighbour in (left, right):
        pl.semaphore_signal(barrier, inc=1, device_id={"patch": neighbour}, device_id_type=MESH)
    for d in range(1, n_lev):
        pl.semaphore_signal(
            barrier, inc=1, device_id={"lev": lax.rem(me + d, n_lev)}, device_id_type=MESH
        )

    if padded > rows:
        edge = rows // SUB * SUB
        xs[edge:padded, :] = jnp.zeros((padded - edge, cells), jnp.float32)
    for t in range(tracers):
        xs[t * own : (t + 1) * own, :] = field[t]

    def copy_to(phase, side):
        return pltpu.make_async_remote_copy(
            src_ref=hsend.at[phase, side],
            dst_ref=hrecv.at[phase, side],
            send_sem=hs_sem.at[phase, side],
            recv_sem=hr_sem.at[phase, side],
            device_id={"patch": left if side else right},
            device_id_type=MESH,
        )

    def meta_to(side):
        return [
            pltpu.make_async_remote_copy(
                src_ref=mine.at[side],
                dst_ref=theirs.at[side],
                send_sem=ms_sem.at[which, side],
                recv_sem=mr_sem.at[which, side],
                device_id={"patch": left if side else right},
                device_id_type=MESH,
            )
            for which, (mine, theirs) in enumerate(((glink, rlink), (gweight, rweight)))
        ]

    def both_sides(step):
        @pl.when(patch == 0)
        def _():
            step(1)
            step(0)

        @pl.when(patch != 0)
        def _():
            step(0)
            step(1)

    outgoing = []

    def scatter(source, base):
        for piece in range(source.shape[1] // chunk):
            d = base // chunk + piece
            part = source.at[:, piece * chunk : (piece + 1) * chunk]
            copy = pltpu.make_async_remote_copy(
                src_ref=part,
                dst_ref=gathered.at[me],
                send_sem=as_sem.at[d],
                recv_sem=ar_sem.at[me],
                device_id={"lev": d},
                device_id_type=MESH,
            )
            outgoing.append((d, copy))

            @pl.when(me != d)
            def _():
                copy.start()

            @pl.when(me == d)
            def _():
                gathered[d] = part[...]

    b1 = n1 // LANES
    b2 = n2 // LANES
    e1 = n1 + 2 * halo1
    e2 = n2 + 2 * halo2
    wide = 256

    def add_tail(into, start, source, depth, high, low, n, add):
        for c in range(0, n, wide):
            cols = slice(start + c, start + c + wide)
            got = product(source, padded, depth, high, low, cols)
            old = into[:, cols]
            into[:, cols] = old + got if add else old - got

    lower = lax.broadcasted_iota(jnp.int32, (padded, LANES), 1) < halo2

    def halo_part(phase, side, value, links, weights, at):
        width = halo2 if phase == 2 else halo1
        start = (n2 if phase == 2 else n1) + side * width
        return reach(value, links.at[at, phase], weights.at[at, phase], start, width)

    def two(send):
        return jnp.concatenate([send[0, 1:2, :], send[0, 0:1, :]], axis=1)

    def share(phase, links, weights, start, blocks, indices):
        for side, index in enumerate(indices):
            picked(links, start, blocks, index, glink.at[side, phase])
            picked(weights, start, blocks, index, gweight.at[side, phase])

    picked(xs, n1, b1, sc1[0, 1:2, :], hsend.at[0, 0])
    picked(xs, n1, b1, sc1[0, 0:1, :], hsend.at[0, 1])
    pl.semaphore_wait(barrier, 2 + n_lev - 1)
    for side in range(2):
        copy_to(0, side).start()
    share(0, pl1, pw1, 0, b1, (sd1[0, 1:2, :], sd1[0, 0:1, :]))
    share(1, ul1, uw1, n2, b2, (two(sc2), two(sc2)))
    share(2, pl2, pw2, 0, b2, (two(sd2), two(sd2)))
    for side in range(2):
        for c in meta_to(side):
            c.start()
    put(ext, padded, 0, xs[:, n1:cells])

    def fine1(cols, got):
        det1[:, cols] = xs[:, cols] - got

    stage(pl1, pw1, merged, 0, n1, b1, e1 // LANES, ext, t1h, t1l, fine1)
    picked(det1, 0, b1, sd1[0, 1:2, :], part.at[0])
    picked(det1, 0, b1, sd1[0, 0:1, :], part.at[1])

    def step0(side):
        copy_to(0, side).wait_recv()
        hsend[1, side] = part[side] - halo_part(0, side, hrecv[0, side], glink, gweight, side)
        copy_to(1, side).start()

    both_sides(step0)
    put(ext, padded, n1, hrecv[0, 0])
    put(ext, padded, n1 + halo1, hrecv[0, 1])
    add_tail(det1, 0, ext, n1, t1h, t1l, n1, False)
    scatter(det1, 0)

    put(ext, padded, 0, det1[...])

    def coarse1(cols, got):
        at = pl.ds(pl.multiple_of(cols.start + n1, LANES), cols.size)
        sm1[:, cols] = xs[:, at] + got

    stage(ul1, uw1, merged, n2, n2, b1, e1 // LANES, ext, t1h, t1l, coarse1)
    picked(sm1, n2, b2, two(sc2), part.at[0])
    picked(det1, 0, b1, sd1[0, 1:2, :], full1.at[0])
    picked(det1, 0, b1, sd1[0, 0:1, :], full1.at[1])
    for side in range(2):
        for c in meta_to(side):
            c.wait_recv()
    for side in range(2):
        early[side] = halo_part(0, 1 - side, hsend[0, 1 - side], rlink, rweight, side)

    def step1(side):
        copy_to(1, side).wait_recv()
        value = hrecv[1, side] - early[side]
        done[side] = value
        hsend[2, side] = part[0] + halo_part(1, side, value, glink, gweight, 0)
        copy_to(2, side).start()

    both_sides(step1)
    put(ext, padded, n1, done[0])
    put(ext, padded, n1 + halo1, done[1])
    add_tail(sm1, n2, ext, n1, t1h, t1l, n2, True)
    put(ext2, padded, 0, sm1[:, n2:n1])

    stage(ul1, uw1, merged, 0, n2, b1, e1 // LANES, ext, t1h, t1l, coarse1)
    add_tail(sm1, 0, ext, n1, t1h, t1l, n2, True)

    def fine2(cols, got):
        det2[:, cols] = sm1[:, cols] - got

    stage(pl2, pw2, merged, 0, n2, b2, e2 // LANES, ext2, t2h, t2l, fine2)
    picked(sm1, n2, b2, two(sc2), full2)
    picked(det2, 0, b2, two(sd2), part.at[1])
    for side in range(2):
        early[side] = halo_part(1, 1 - side, full1[1 - side], rlink, rweight, side)

    def step2(side):
        copy_to(2, side).wait_recv()
        value = hrecv[2, side] + early[side]
        done[side] = value
        hsend[3, side] = part[1] - halo_part(2, side, value, glink, gweight, 0)
        copy_to(3, side).start()

    both_sides(step2)
    put(ext2, padded, n2, jnp.where(lower, done[0], done[1]))
    add_tail(det2, 0, ext2, n2, t2h, t2l, n2, False)
    scatter(det2, n1)

    put(ext2, padded, 0, det2[...])

    def coarse2(cols, got):
        at = pl.ds(pl.multiple_of(cols.start + n2, LANES), cols.size)
        sm2[:, cols] = sm1[:, at] + got

    stage(ul2, uw2, merged, 0, n2, b2, e2 // LANES, ext2, t2h, t2l, coarse2)
    for side in range(2):
        early[side] = halo_part(2, 1 - side, full2[...], rlink, rweight, side)

    def step3(side):
        copy_to(3, side).wait_recv()
        done[side] = hrecv[3, side] - early[side]

    both_sides(step3)
    put(ext2, padded, n2, jnp.where(lower, done[0], done[1]))
    add_tail(sm2, 0, ext2, n2, t2h, t2l, n2, True)
    scatter(sm2, n1 + n2)

    for s in range(n_lev):

        @pl.when(me != s)
        def _():
            pltpu.make_async_remote_copy(
                src_ref=gathered.at[s],
                dst_ref=gathered.at[s],
                send_sem=as_sem.at[s],
                recv_sem=ar_sem.at[s],
                device_id={"lev": s},
                device_id_type=MESH,
            ).wait_recv()

    for side in range(2):
        for phase in range(4):
            copy_to(phase, side).wait_send()
        for c in meta_to(side):
            c.wait_send()
    for d, copy in outgoing:

        @pl.when(me != d)
        def _():
            copy.wait_send()


def transform(gathered, t_high, t_low, out):
    groups, padded, chunk = gathered.shape
    tracers, levels, _ = out.shape
    high, low = halves(gathered[...].reshape(groups * padded, chunk))
    for t in range(tracers):
        rows = slice(t * levels, (t + 1) * levels)
        out[t] = (
            jnp.dot(t_high[rows, :], high, preferred_element_type=jnp.float32)
            + jnp.dot(t_high[rows, :], low, preferred_element_type=jnp.float32)
            + jnp.dot(t_low[rows, :], high, preferred_element_type=jnp.float32)
        )


def on_device(n_patch, n_lev, *args):
    field, sc1 = args[0], args[1]
    own, tracers, cells = field.shape
    levels = own * n_lev
    rows = own * tracers
    padded = -(-rows // (2 * SUB)) * (2 * SUB)
    n1, n2 = cells // 2, cells // 4
    e1 = n1 + 2 * sc1.shape[2]
    e2 = n2 + 2 * args[3].shape[2]
    chunk = cells // n_lev
    slots = args[5].shape[0]
    t_high, t_low = spread_table(levels, tracers, n_lev, padded)
    f32, bf16 = jnp.float32, jnp.bfloat16
    gathered = pl.pallas_call(
        functools.partial(body, n_patch, n_lev, levels),
        out_shape=jax.ShapeDtypeStruct((n_lev, padded, chunk), f32),
        in_specs=[pl.BlockSpec(memory_space=pltpu.VMEM)] * 13,
        out_specs=pl.BlockSpec(memory_space=pltpu.VMEM),
        scratch_shapes=[
            pltpu.VMEM((padded, cells), f32),
            pltpu.VMEM((2 * padded, e1), bf16),
            pltpu.VMEM((2, slots, -(-(e1 // LANES) // SUB) * SUB, LANES), f32),
            pltpu.VMEM((e1 - n1, n1), bf16),
            pltpu.VMEM((e1 - n1, n1), bf16),
            pltpu.VMEM((e2 - n2, n2), bf16),
            pltpu.VMEM((e2 - n2, n2), bf16),
            pltpu.VMEM((padded, n1), f32),
            pltpu.VMEM((padded, n1), f32),
            pltpu.VMEM((padded, n2), f32),
            pltpu.VMEM((padded, n2), f32),
            pltpu.VMEM((4, 2, padded, LANES), f32),
            pltpu.VMEM((4, 2, padded, LANES), f32),
            pltpu.VMEM((2 * padded, e2), bf16),
            pltpu.VMEM((2, 3, slots, LANES), jnp.int32),
            pltpu.VMEM((2, 3, slots, LANES), f32),
            pltpu.VMEM((2, 3, slots, LANES), jnp.int32),
            pltpu.VMEM((2, 3, slots, LANES), f32),
            pltpu.VMEM((2, padded, LANES), f32),
            pltpu.VMEM((2, padded, LANES), f32),
            pltpu.VMEM((padded, LANES), f32),
            pltpu.VMEM((2, padded, LANES), f32),
            pltpu.VMEM((2, padded, LANES), f32),
            pltpu.SemaphoreType.DMA((2, 2)),
            pltpu.SemaphoreType.DMA((2, 2)),
            pltpu.SemaphoreType.DMA((4, 2)),
            pltpu.SemaphoreType.DMA((4, 2)),
            pltpu.SemaphoreType.DMA((n_lev,)),
            pltpu.SemaphoreType.DMA((n_lev,)),
        ],
        compiler_params=pltpu.CompilerParams(collective_id=0, has_side_effects=True),
    )(jnp.transpose(field, (1, 0, 2)), *args[1:])
    result = pl.pallas_call(
        transform,
        out_shape=jax.ShapeDtypeStruct((tracers, levels, chunk), f32),
        in_specs=[pl.BlockSpec(memory_space=pltpu.VMEM)] * 3,
        out_specs=pl.BlockSpec(memory_space=pltpu.VMEM),
    )(gathered, jnp.asarray(t_high), jnp.asarray(t_low))
    return jnp.transpose(result, (1, 0, 2))


def solution(mesh):
    in_specs = (P("lev", None, "patch"),)
    in_specs += (P("patch", None, None),) * 4
    in_specs += (P(None, "patch"),) * 8
    out_specs = P(None, None, ("patch", "lev"))
    fn = functools.partial(on_device, mesh.shape["patch"], mesh.shape["lev"])
    return jax.shard_map(
        fn, mesh=mesh, in_specs=in_specs, out_specs=out_specs, check_vma=False
    )
```

```python
import functools

import jax
import jax.numpy as jnp
import ml_dtypes
import numpy as np
from jax import lax
from jax.experimental import pallas as pl
from jax.experimental.pallas import tpu as pltpu
from jax.sharding import PartitionSpec as P

LANES = 128
SUB = 8
MESH = pl.DeviceIdType.MESH


def cosine_table(length):
    rows = np.arange(length, dtype=np.float64)[:, None]
    columns = np.arange(length, dtype=np.float64)[None, :]
    matrix = np.cos(np.pi * (columns + 0.5) * rows / length) * np.sqrt(2.0 / length)
    matrix[0] *= np.sqrt(0.5)
    return matrix


def spread_table(levels, tracers, groups, padded):
    own = levels // groups
    table = cosine_table(levels).reshape(levels, groups, own)
    wide = np.zeros((tracers, levels, groups, padded))
    for t in range(tracers):
        wide[t, :, :, t * own : (t + 1) * own] = table
    wide = wide.reshape(levels * tracers, groups * padded).astype(np.float32)
    high = wide.astype(ml_dtypes.bfloat16)
    low = (wide - high.astype(np.float32)).astype(ml_dtypes.bfloat16)
    return high, low


def halves(x):
    high = x.astype(jnp.bfloat16)
    low = (x - high.astype(jnp.float32)).astype(jnp.bfloat16)
    return high, low


def along(table, index):
    numbers = lax.GatherDimensionNumbers(
        offset_dims=(),
        collapsed_slice_dims=(0,),
        start_index_map=(0,),
        operand_batching_dims=(1,),
        start_indices_batching_dims=(1,),
    )
    mode = lax.GatherScatterMode.PROMISE_IN_BOUNDS
    return lax.gather(table, index[:, :, None], numbers, (1, 1), mode=mode)


def tile(links, weights, merged, cols, blocks):
    slots = links.shape[0]
    lane = []
    block = []
    weight = []
    for k in range(slots):
        link = jnp.broadcast_to(links[k : k + 1, cols], (SUB, LANES))
        lane.append(link & (LANES - 1))
        block.append(link >> 7)
        weight.append(jnp.broadcast_to(weights[k : k + 1, cols], (SUB, LANES)))
    which = lax.broadcasted_iota(jnp.int32, (SUB, LANES), 0)
    same = [[lane[j] == lane[k] for j in range(k)] for k in range(slots)]
    for g in range(-(-blocks // SUB)):
        placed = []
        for k in range(slots):
            mine = jnp.where(block[k] == which + g * SUB, weight[k], 0.0)
            total = mine
            for j in range(k):
                total = total + jnp.where(same[k][j], placed[j], 0.0)
            placed.append(mine)
            merged[k, g * SUB : (g + 1) * SUB, :] = total
    none = jnp.zeros((2 * SUB - slots, LANES), jnp.float32)
    tables = [halves(jnp.concatenate([merged[:, b, :], none], axis=0)) for b in range(blocks)]
    short = [jnp.concatenate([v, v], axis=0).astype(jnp.int16) for v in lane]
    strips = []
    for s in range(LANES // (2 * SUB)):
        rows = lax.broadcasted_iota(jnp.int16, (2 * SUB, LANES), 0) + jnp.int16(s * 2 * SUB)
        index = jnp.full((2 * SUB, LANES), slots, jnp.int16)
        for k in range(slots):
            index = jnp.where(short[k] == rows, jnp.int16(k), index)
        strips.append(index)
    return tables, strips


def spread(tiles, part, first, last):
    return jnp.concatenate(
        [
            jnp.concatenate(
                [along(tables[b][part], index) for b in range(first, last) for index in strips],
                axis=0,
            )
            for tables, strips in tiles
        ],
        axis=1,
    )


def stage(links, weights, merged, first, count, own, blocks, ext, tail_high, tail_low, emit):
    padded = ext.shape[0] // 2
    depth = own * LANES

    def step(t, _):
        start = pl.multiple_of(first + t * 2 * LANES, 2 * LANES)
        tiles = [
            tile(
                links, weights, merged.at[h],
                pl.ds(pl.multiple_of(start + h * LANES, LANES), LANES), blocks,
            )
            for h in range(2)
        ]
        high = spread(tiles, 0, 0, own)
        low = spread(tiles, 1, 0, own)
        both = jnp.dot(ext[:, 0:depth], high, preferred_element_type=jnp.float32)
        rest = jnp.dot(ext[0:padded, 0:depth], low, preferred_element_type=jnp.float32)
        cols = pl.ds(start, 2 * LANES)
        emit(cols, both[0:padded] + both[padded : 2 * padded] + rest)
        tail_high[:, cols] = spread(tiles, 0, own, blocks)
        tail_low[:, cols] = spread(tiles, 1, own, blocks)
        return 0

    lax.fori_loop(0, count // (2 * LANES), step, 0)


def picked(source, start, blocks, index, out):
    lane = jnp.broadcast_to(index & (LANES - 1), (SUB, LANES))
    block = jnp.broadcast_to(index >> 7, (SUB, LANES))
    for r in range(source.shape[0] // SUB):
        rows = slice(r * SUB, (r + 1) * SUB)
        got = None
        for b in range(blocks):
            cols = slice(start + b * LANES, start + (b + 1) * LANES)
            t = jnp.take_along_axis(source[rows, cols], lane, axis=1)
            got = t if got is None else jnp.where(block == b, t, got)
        out[rows, :] = got


def put(ext, padded, at, value):
    high, low = halves(value)
    width = value.shape[1]
    ext[0:padded, at : at + width] = high
    ext[padded : 2 * padded, at : at + width] = low


def product(ext, padded, start, w_high, w_low, cols):
    k = slice(start, start + w_high.shape[0])
    both = jnp.dot(ext[:, k], w_high[:, cols], preferred_element_type=jnp.float32)
    rest = jnp.dot(ext[0:padded, k], w_low[:, cols], preferred_element_type=jnp.float32)
    return both[0:padded] + both[padded : 2 * padded] + rest


def reach(value, links, weights, start, width):
    padded = value.shape[0]
    rows = [value[r * SUB : (r + 1) * SUB, :] for r in range(padded // SUB)]
    totals = [None] * len(rows)
    for k in range(links.shape[0]):
        link = jnp.broadcast_to(links[k : k + 1, :], (SUB, LANES))
        weight = jnp.broadcast_to(weights[k : k + 1, :], (SUB, LANES))
        weight = jnp.where((link >= start) & (link < start + width), weight, 0.0)
        lane = link & (LANES - 1)
        for r, row in enumerate(rows):
            term = weight * jnp.take_along_axis(row, lane, axis=1)
            totals[r] = term if totals[r] is None else totals[r] + term
    return jnp.concatenate(totals, axis=0)


def body(
    n_patch, n_lev, levels,
    *refs,
):
    given, gathered, held, rest = refs[:13], refs[13], refs[14:27], refs[27:]
    field, sc1, sd1, sc2, sd2, pl1, pw1, ul1, uw1, pl2, pw2, ul2, uw2 = held
    (
    xs, ext, merged, t1h, t1l, t2h, t2l,
    det1, sm1, det2, sm2, hsend, hrecv,
    ext2, glink, gweight, rlink, rweight, part, full1, full2, done, early,
    ms_sem, mr_sem,
    hs_sem, hr_sem, as_sem, ar_sem, in_sem,
    ) = rest
    tracers, own, cells = field.shape
    rows = own * tracers
    padded = xs.shape[0]
    n1 = cells // 2
    n2 = cells // 4
    halo1 = sc1.shape[2]
    halo2 = sc2.shape[2]
    chunk = cells // n_lev
    me = lax.axis_index("lev")
    patch = lax.axis_index("patch")
    left = lax.rem(patch + n_patch - 1, n_patch)
    right = lax.rem(patch + 1, n_patch)

    barrier = pltpu.get_barrier_semaphore()
    for neighbour in (left, right):
        pl.semaphore_signal(barrier, inc=1, device_id={"patch": neighbour}, device_id_type=MESH)
    for d in range(1, n_lev):
        pl.semaphore_signal(
            barrier, inc=1, device_id={"lev": lax.rem(me + d, n_lev)}, device_id_type=MESH
        )

    coarse = (slice(None), slice(None), slice(n1, cells))
    fine = (slice(None), slice(None), slice(0, n1))
    loads = {0: pltpu.make_async_copy(given[0].at[coarse], field.at[coarse], in_sem.at[0])}
    for i in (1, 5, 6, 2):
        loads[i] = pltpu.make_async_copy(given[i], held[i], in_sem.at[i])
    loads[13] = pltpu.make_async_copy(given[0].at[fine], field.at[fine], in_sem.at[13])
    for i in (3, 4, 7, 8, 9, 10, 11, 12):
        loads[i] = pltpu.make_async_copy(given[i], held[i], in_sem.at[i])
    for load in loads.values():
        load.start()

    def pack(start, stop):
        if padded > rows:
            edge = rows // SUB * SUB
            xs[edge:padded, start:stop] = jnp.zeros((padded - edge, stop - start), jnp.float32)
        for t in range(tracers):
            xs[t * own : (t + 1) * own, start:stop] = field[t, :, start:stop]

    loads.pop(0).wait()
    loads.pop(1).wait()
    pack(n1, cells)

    def copy_to(phase, side):
        return pltpu.make_async_remote_copy(
            src_ref=hsend.at[phase, side],
            dst_ref=hrecv.at[phase, side],
            send_sem=hs_sem.at[phase, side],
            recv_sem=hr_sem.at[phase, side],
            device_id={"patch": left if side else right},
            device_id_type=MESH,
        )

    def meta_to(side):
        return [
            pltpu.make_async_remote_copy(
                src_ref=mine.at[side],
                dst_ref=theirs.at[side],
                send_sem=ms_sem.at[which, side],
                recv_sem=mr_sem.at[which, side],
                device_id={"patch": left if side else right},
                device_id_type=MESH,
            )
            for which, (mine, theirs) in enumerate(((glink, rlink), (gweight, rweight)))
        ]

    def both_sides(step):
        @pl.when(patch == 0)
        def _():
            step(1)
            step(0)

        @pl.when(patch != 0)
        def _():
            step(0)
            step(1)

    outgoing = []

    def scatter(source, base):
        for piece in range(source.shape[1] // chunk):
            d = base // chunk + piece
            part = source.at[:, piece * chunk : (piece + 1) * chunk]
            copy = pltpu.make_async_remote_copy(
                src_ref=part,
                dst_ref=gathered.at[me],
                send_sem=as_sem.at[d],
                recv_sem=ar_sem.at[me],
                device_id={"lev": d},
                device_id_type=MESH,
            )
            outgoing.append((d, copy))

            @pl.when(me != d)
            def _():
                copy.start()

            @pl.when(me == d)
            def _():
                gathered[d] = part[...]

    b1 = n1 // LANES
    b2 = n2 // LANES
    e1 = n1 + 2 * halo1
    e2 = n2 + 2 * halo2
    wide = 256

    def add_tail(into, start, source, depth, high, low, n, add):
        for c in range(0, n, wide):
            cols = slice(start + c, start + c + wide)
            got = product(source, padded, depth, high, low, cols)
            old = into[:, cols]
            into[:, cols] = old + got if add else old - got

    lower = lax.broadcasted_iota(jnp.int32, (padded, LANES), 1) < halo2

    def halo_part(phase, side, value, links, weights, at):
        width = halo2 if phase == 2 else halo1
        start = (n2 if phase == 2 else n1) + side * width
        return reach(value, links.at[at, phase], weights.at[at, phase], start, width)

    def two(send):
        return jnp.concatenate([send[0, 1:2, :], send[0, 0:1, :]], axis=1)

    def share(phase, links, weights, start, blocks, indices):
        for side, index in enumerate(indices):
            picked(links, start, blocks, index, glink.at[side, phase])
            picked(weights, start, blocks, index, gweight.at[side, phase])

    picked(xs, n1, b1, sc1[0, 1:2, :], hsend.at[0, 0])
    picked(xs, n1, b1, sc1[0, 0:1, :], hsend.at[0, 1])
    pl.semaphore_wait(barrier, 2 + n_lev - 1)
    for side in range(2):
        copy_to(0, side).start()
    for load in loads.values():
        load.wait()
    pack(0, n1)
    share(0, pl1, pw1, 0, b1, (sd1[0, 1:2, :], sd1[0, 0:1, :]))
    share(1, ul1, uw1, n2, b2, (two(sc2), two(sc2)))
    share(2, pl2, pw2, 0, b2, (two(sd2), two(sd2)))
    for side in range(2):
        for c in meta_to(side):
            c.start()
    put(ext, padded, 0, xs[:, n1:cells])

    def fine1(cols, got):
        det1[:, cols] = xs[:, cols] - got

    stage(pl1, pw1, merged, 0, n1, b1, e1 // LANES, ext, t1h, t1l, fine1)
    picked(det1, 0, b1, sd1[0, 1:2, :], part.at[0])
    picked(det1, 0, b1, sd1[0, 0:1, :], part.at[1])

    def step0(side):
        copy_to(0, side).wait_recv()
        hsend[1, side] = part[side] - halo_part(0, side, hrecv[0, side], glink, gweight, side)
        copy_to(1, side).start()

    both_sides(step0)
    put(ext, padded, n1, hrecv[0, 0])
    put(ext, padded, n1 + halo1, hrecv[0, 1])
    add_tail(det1, 0, ext, n1, t1h, t1l, n1, False)
    scatter(det1, 0)

    put(ext, padded, 0, det1[...])

    def coarse1(cols, got):
        at = pl.ds(pl.multiple_of(cols.start + n1, LANES), cols.size)
        sm1[:, cols] = xs[:, at] + got

    stage(ul1, uw1, merged, n2, n2, b1, e1 // LANES, ext, t1h, t1l, coarse1)
    picked(sm1, n2, b2, two(sc2), part.at[0])
    picked(det1, 0, b1, sd1[0, 1:2, :], full1.at[0])
    picked(det1, 0, b1, sd1[0, 0:1, :], full1.at[1])
    for side in range(2):
        for c in meta_to(side):
            c.wait_recv()
    for side in range(2):
        early[side] = halo_part(0, 1 - side, hsend[0, 1 - side], rlink, rweight, side)

    def step1(side):
        copy_to(1, side).wait_recv()
        value = hrecv[1, side] - early[side]
        done[side] = value
        hsend[2, side] = part[0] + halo_part(1, side, value, glink, gweight, 0)
        copy_to(2, side).start()

    both_sides(step1)
    put(ext, padded, n1, done[0])
    put(ext, padded, n1 + halo1, done[1])
    add_tail(sm1, n2, ext, n1, t1h, t1l, n2, True)
    put(ext2, padded, 0, sm1[:, n2:n1])

    stage(ul1, uw1, merged, 0, n2, b1, e1 // LANES, ext, t1h, t1l, coarse1)
    add_tail(sm1, 0, ext, n1, t1h, t1l, n2, True)

    def fine2(cols, got):
        det2[:, cols] = sm1[:, cols] - got

    stage(pl2, pw2, merged, 0, n2, b2, e2 // LANES, ext2, t2h, t2l, fine2)
    picked(sm1, n2, b2, two(sc2), full2)
    picked(det2, 0, b2, two(sd2), part.at[1])
    for side in range(2):
        early[side] = halo_part(1, 1 - side, full1[1 - side], rlink, rweight, side)

    def step2(side):
        copy_to(2, side).wait_recv()
        value = hrecv[2, side] + early[side]
        done[side] = value
        hsend[3, side] = part[1] - halo_part(2, side, value, glink, gweight, 0)
        copy_to(3, side).start()

    both_sides(step2)
    put(ext2, padded, n2, jnp.where(lower, done[0], done[1]))
    add_tail(det2, 0, ext2, n2, t2h, t2l, n2, False)
    scatter(det2, n1)

    put(ext2, padded, 0, det2[...])

    def coarse2(cols, got):
        at = pl.ds(pl.multiple_of(cols.start + n2, LANES), cols.size)
        sm2[:, cols] = sm1[:, at] + got

    stage(ul2, uw2, merged, 0, n2, b2, e2 // LANES, ext2, t2h, t2l, coarse2)
    for side in range(2):
        early[side] = halo_part(2, 1 - side, full2[...], rlink, rweight, side)

    def step3(side):
        copy_to(3, side).wait_recv()
        done[side] = hrecv[3, side] - early[side]

    both_sides(step3)
    put(ext2, padded, n2, jnp.where(lower, done[0], done[1]))
    add_tail(sm2, 0, ext2, n2, t2h, t2l, n2, True)
    scatter(sm2, n1 + n2)

    for s in range(n_lev):

        @pl.when(me != s)
        def _():
            pltpu.make_async_remote_copy(
                src_ref=gathered.at[s],
                dst_ref=gathered.at[s],
                send_sem=as_sem.at[s],
                recv_sem=ar_sem.at[s],
                device_id={"lev": s},
                device_id_type=MESH,
            ).wait_recv()

    for side in range(2):
        for phase in range(4):
            copy_to(phase, side).wait_send()
        for c in meta_to(side):
            c.wait_send()
    for d, copy in outgoing:

        @pl.when(me != d)
        def _():
            copy.wait_send()


def transform(gathered, t_high, t_low, out):
    groups, padded, chunk = gathered.shape
    tracers, levels, _ = out.shape
    high, low = halves(gathered[...].reshape(groups * padded, chunk))
    for t in range(tracers):
        rows = slice(t * levels, (t + 1) * levels)
        out[t] = (
            jnp.dot(t_high[rows, :], high, preferred_element_type=jnp.float32)
            + jnp.dot(t_high[rows, :], low, preferred_element_type=jnp.float32)
            + jnp.dot(t_low[rows, :], high, preferred_element_type=jnp.float32)
        )


def on_device(n_patch, n_lev, *args):
    field, sc1 = args[0], args[1]
    own, tracers, cells = field.shape
    levels = own * n_lev
    rows = own * tracers
    padded = -(-rows // (2 * SUB)) * (2 * SUB)
    n1, n2 = cells // 2, cells // 4
    e1 = n1 + 2 * sc1.shape[2]
    e2 = n2 + 2 * args[3].shape[2]
    chunk = cells // n_lev
    slots = args[5].shape[0]
    t_high, t_low = spread_table(levels, tracers, n_lev, padded)
    f32, bf16 = jnp.float32, jnp.bfloat16
    gathered = pl.pallas_call(
        functools.partial(body, n_patch, n_lev, levels),
        out_shape=jax.ShapeDtypeStruct((n_lev, padded, chunk), f32),
        in_specs=[pl.BlockSpec(memory_space=pltpu.HBM)] * 13,
        out_specs=pl.BlockSpec(memory_space=pltpu.VMEM),
        scratch_shapes=[
            pltpu.VMEM((tracers, own, cells), f32),
            *(pltpu.VMEM(a.shape, a.dtype) for a in args[1:]),
            pltpu.VMEM((padded, cells), f32),
            pltpu.VMEM((2 * padded, e1), bf16),
            pltpu.VMEM((2, slots, -(-(e1 // LANES) // SUB) * SUB, LANES), f32),
            pltpu.VMEM((e1 - n1, n1), bf16),
            pltpu.VMEM((e1 - n1, n1), bf16),
            pltpu.VMEM((e2 - n2, n2), bf16),
            pltpu.VMEM((e2 - n2, n2), bf16),
            pltpu.VMEM((padded, n1), f32),
            pltpu.VMEM((padded, n1), f32),
            pltpu.VMEM((padded, n2), f32),
            pltpu.VMEM((padded, n2), f32),
            pltpu.VMEM((4, 2, padded, LANES), f32),
            pltpu.VMEM((4, 2, padded, LANES), f32),
            pltpu.VMEM((2 * padded, e2), bf16),
            pltpu.VMEM((2, 3, slots, LANES), jnp.int32),
            pltpu.VMEM((2, 3, slots, LANES), f32),
            pltpu.VMEM((2, 3, slots, LANES), jnp.int32),
            pltpu.VMEM((2, 3, slots, LANES), f32),
            pltpu.VMEM((2, padded, LANES), f32),
            pltpu.VMEM((2, padded, LANES), f32),
            pltpu.VMEM((padded, LANES), f32),
            pltpu.VMEM((2, padded, LANES), f32),
            pltpu.VMEM((2, padded, LANES), f32),
            pltpu.SemaphoreType.DMA((2, 2)),
            pltpu.SemaphoreType.DMA((2, 2)),
            pltpu.SemaphoreType.DMA((4, 2)),
            pltpu.SemaphoreType.DMA((4, 2)),
            pltpu.SemaphoreType.DMA((n_lev,)),
            pltpu.SemaphoreType.DMA((n_lev,)),
            pltpu.SemaphoreType.DMA((14,)),
        ],
        compiler_params=pltpu.CompilerParams(
            collective_id=0, has_side_effects=True, vmem_limit_bytes=16 << 20
        ),
    )(*(pltpu.with_memory_space_constraint(a, pltpu.HBM) for a in (jnp.transpose(field, (1, 0, 2)), *args[1:])))
    result = pl.pallas_call(
        transform,
        out_shape=jax.ShapeDtypeStruct((tracers, levels, chunk), f32),
        in_specs=[pl.BlockSpec(memory_space=pltpu.VMEM)] * 3,
        out_specs=pl.BlockSpec(memory_space=pltpu.VMEM),
        compiler_params=pltpu.CompilerParams(vmem_limit_bytes=8 << 20),
    )(gathered, jnp.asarray(t_high), jnp.asarray(t_low))
    return jnp.transpose(result, (1, 0, 2))


def solution(mesh):
    in_specs = (P("lev", None, "patch"),)
    in_specs += (P("patch", None, None),) * 4
    in_specs += (P(None, "patch"),) * 8
    out_specs = P(None, None, ("patch", "lev"))
    fn = functools.partial(on_device, mesh.shape["patch"], mesh.shape["lev"])
    return jax.shard_map(
        fn, mesh=mesh, in_specs=in_specs, out_specs=out_specs, check_vma=False
    )
```

```python
import functools

import jax
import jax.numpy as jnp
import ml_dtypes
import numpy as np
from jax import lax
from jax.experimental import pallas as pl
from jax.experimental.pallas import tpu as pltpu
from jax.sharding import PartitionSpec as P

LANES = 128
SUB = 8
MESH = pl.DeviceIdType.MESH


def cosine_table(length):
    rows = np.arange(length, dtype=np.float64)[:, None]
    columns = np.arange(length, dtype=np.float64)[None, :]
    matrix = np.cos(np.pi * (columns + 0.5) * rows / length) * np.sqrt(2.0 / length)
    matrix[0] *= np.sqrt(0.5)
    return matrix


def spread_table(levels, tracers, groups, padded):
    own = levels // groups
    table = cosine_table(levels).reshape(levels, groups, own)
    wide = np.zeros((tracers, levels, groups, padded))
    for t in range(tracers):
        wide[t, :, :, t * own : (t + 1) * own] = table
    wide = wide.reshape(levels * tracers, groups * padded).astype(np.float32)
    high = wide.astype(ml_dtypes.bfloat16)
    low = (wide - high.astype(np.float32)).astype(ml_dtypes.bfloat16)
    return high, low


def halves(x):
    high = x.astype(jnp.bfloat16)
    low = (x - high.astype(jnp.float32)).astype(jnp.bfloat16)
    return high, low


def along(table, index):
    numbers = lax.GatherDimensionNumbers(
        offset_dims=(),
        collapsed_slice_dims=(0,),
        start_index_map=(0,),
        operand_batching_dims=(1,),
        start_indices_batching_dims=(1,),
    )
    mode = lax.GatherScatterMode.PROMISE_IN_BOUNDS
    return lax.gather(table, index[:, :, None], numbers, (1, 1), mode=mode)


def tile(links, weights, merged, cols, blocks):
    slots = links.shape[0]
    lane = []
    block = []
    weight = []
    for k in range(slots):
        link = jnp.broadcast_to(links[k : k + 1, cols], (SUB, LANES))
        lane.append(link & (LANES - 1))
        block.append(link >> 7)
        weight.append(jnp.broadcast_to(weights[k : k + 1, cols], (SUB, LANES)))
    which = lax.broadcasted_iota(jnp.int32, (SUB, LANES), 0)
    same = [[lane[j] == lane[k] for j in range(k)] for k in range(slots)]
    for g in range(-(-blocks // SUB)):
        placed = []
        for k in range(slots):
            mine = jnp.where(block[k] == which + g * SUB, weight[k], 0.0)
            total = mine
            for j in range(k):
                total = total + jnp.where(same[k][j], placed[j], 0.0)
            placed.append(mine)
            merged[k, g * SUB : (g + 1) * SUB, :] = total
    none = jnp.zeros((2 * SUB - slots, LANES), jnp.float32)
    tables = [halves(jnp.concatenate([merged[:, b, :], none], axis=0)) for b in range(blocks)]
    short = [jnp.concatenate([v, v], axis=0).astype(jnp.int16) for v in lane]
    strips = []
    for s in range(LANES // (2 * SUB)):
        rows = lax.broadcasted_iota(jnp.int16, (2 * SUB, LANES), 0) + jnp.int16(s * 2 * SUB)
        index = jnp.full((2 * SUB, LANES), slots, jnp.int16)
        for k in range(slots):
            index = jnp.where(short[k] == rows, jnp.int16(k), index)
        strips.append(index)
    return tables, strips


def spread(tiles, part, first, last):
    return jnp.concatenate(
        [
            jnp.concatenate(
                [along(tables[b][part], index) for b in range(first, last) for index in strips],
                axis=0,
            )
            for tables, strips in tiles
        ],
        axis=1,
    )


def stage(links, weights, merged, first, count, own, blocks, ext, tail, emit):
    padded = ext.shape[0] // 2
    depth = own * LANES
    width = min(count, 2 * LANES)

    def step(t, _):
        start = pl.multiple_of(first + t * width, width)
        tiles = [
            tile(
                links, weights, merged.at[h],
                pl.ds(pl.multiple_of(start + h * LANES, LANES), LANES), blocks,
            )
            for h in range(width // LANES)
        ]
        high = spread(tiles, 0, 0, own)
        low = spread(tiles, 1, 0, own)
        both = jnp.dot(ext[:, 0:depth], high, preferred_element_type=jnp.float32)
        rest = jnp.dot(ext[0:padded, 0:depth], low, preferred_element_type=jnp.float32)
        cols = pl.ds(start, width)
        emit(cols, both[0:padded] + both[padded : 2 * padded] + rest)
        if tail is not None:
            tail[0][:, cols] = spread(tiles, 0, own, blocks)
            tail[1][:, cols] = spread(tiles, 1, own, blocks)
        return 0

    lax.fori_loop(0, count // width, step, 0)


def prepare(links, weights, merged, count, blocks, out):
    def step(t, _):
        cols = pl.ds(pl.multiple_of(t * LANES, LANES), LANES)
        tiles = [tile(links, weights, merged.at[0], cols, blocks)]
        out[0][:, cols] = spread(tiles, 0, 0, blocks)
        out[1][:, cols] = spread(tiles, 1, 0, blocks)
        return 0

    lax.fori_loop(0, count // LANES, step, 0)


def picked(source, start, blocks, index, out):
    lane = jnp.broadcast_to(index & (LANES - 1), (SUB, LANES))
    block = jnp.broadcast_to(index >> 7, (SUB, LANES))
    for r in range(source.shape[0] // SUB):
        rows = slice(r * SUB, (r + 1) * SUB)
        got = None
        for b in range(blocks):
            cols = slice(start + b * LANES, start + (b + 1) * LANES)
            t = jnp.take_along_axis(source[rows, cols], lane, axis=1)
            got = t if got is None else jnp.where(block == b, t, got)
        out[rows, :] = got


def put(ext, padded, at, value):
    high, low = halves(value)
    width = value.shape[1]
    ext[0:padded, at : at + width] = high
    ext[padded : 2 * padded, at : at + width] = low


def product(ext, padded, start, w_high, w_low, cols):
    k = slice(start, start + w_high.shape[0])
    both = jnp.dot(ext[:, k], w_high[:, cols], preferred_element_type=jnp.float32)
    rest = jnp.dot(ext[0:padded, k], w_low[:, cols], preferred_element_type=jnp.float32)
    return both[0:padded] + both[padded : 2 * padded] + rest


def reach(value, links, weights, keep):
    padded = value.shape[0]
    rows = [value[r * SUB : (r + 1) * SUB, :] for r in range(padded // SUB)]
    totals = [None] * len(rows)
    for k in range(links.shape[0]):
        link = jnp.broadcast_to(links[k : k + 1, :], (SUB, LANES))
        weight = jnp.broadcast_to(weights[k : k + 1, :], (SUB, LANES))
        weight = jnp.where(keep(link), weight, 0.0)
        lane = link & (LANES - 1)
        for r, row in enumerate(rows):
            term = weight * jnp.take_along_axis(row, lane, axis=1)
            totals[r] = term if totals[r] is None else totals[r] + term
    return jnp.concatenate(totals, axis=0)


def body(n_patch, n_lev, levels, *refs):
    given, gathered, held, rest = refs[:13], refs[13], refs[14:27], refs[27:]
    field, sc1, sd1, sc2, sd2, pl1, pw1, ul1, uw1, pl2, pw2, ul2, uw2 = held
    (
        xs, ext, ext2, merged, t1h, t1l, t2h, t2l, w2h, w2l,
        det1, sm1, det2, sm2,
        asend, arecv, afar, bsend, brecv, csend, crecv, cfar,
        link1, weight1, link2, weight2, link3, weight3, rlink1, rweight1, rlink2, rweight2,
        fpart, own2, early1, early2, hsend, hrecv,
        in_sem, x_send, x_recv, m_send, m_recv, g_send, g_recv, h_send, h_recv,
    ) = rest
    tracers, own, cells = field.shape
    rows = own * tracers
    padded = xs.shape[0]
    n1 = cells // 2
    n2 = cells // 4
    halo1 = sc1.shape[2]
    halo2 = sc2.shape[2]
    chunk = cells // n_lev
    b1 = n1 // LANES
    b2 = n2 // LANES
    e1 = n1 + 2 * halo1
    e2 = n2 + 2 * halo2
    wide = 256
    me = lax.axis_index("lev")
    patch = lax.axis_index("patch")

    def away(steps):
        return lax.rem(patch + n_patch + steps, n_patch)

    barrier = pltpu.get_barrier_semaphore()
    for steps in (-2, -1, 1, 2):
        pl.semaphore_signal(barrier, inc=1, device_id={"patch": away(steps)}, device_id_type=MESH)
    for d in range(1, n_lev):
        pl.semaphore_signal(
            barrier, inc=1, device_id={"lev": lax.rem(me + d, n_lev)}, device_id_type=MESH
        )

    coarse = (slice(None), slice(None), slice(n1, cells))
    fine = (slice(None), slice(None), slice(0, n1))
    loads = {0: pltpu.make_async_copy(given[0].at[coarse], field.at[coarse], in_sem.at[0])}
    for i in (1, 5, 6, 2):
        loads[i] = pltpu.make_async_copy(given[i], held[i], in_sem.at[i])
    loads[13] = pltpu.make_async_copy(given[0].at[fine], field.at[fine], in_sem.at[13])
    for i in (3, 4, 7, 8, 9, 10, 11, 12):
        loads[i] = pltpu.make_async_copy(given[i], held[i], in_sem.at[i])
    for load in loads.values():
        load.start()

    def loaded(*which):
        for i in which:
            loads[i].wait()

    def pack(start, stop):
        if padded > rows:
            edge = rows // SUB * SUB
            xs[edge:padded, start:stop] = jnp.zeros((padded - edge, stop - start), jnp.float32)
        for t in range(tracers):
            xs[t * own : (t + 1) * own, start:stop] = field[t, :, start:stop]

    def message(which, side, steps, source, target):
        return pltpu.make_async_remote_copy(
            src_ref=source.at[side],
            dst_ref=target.at[side],
            send_sem=x_send.at[which, side],
            recv_sem=x_recv.at[which, side],
            device_id={"patch": away(-steps if side else steps)},
            device_id_type=MESH,
        )

    near1 = [message(0, side, 1, asend, arecv) for side in range(2)]
    far1 = [message(1, side, 2, asend, afar) for side in range(2)]
    part1 = [message(2, side, 1, bsend, brecv) for side in range(2)]
    near2 = [message(3, side, 1, csend, crecv) for side in range(2)]
    far2 = [message(4, side, 2, csend, cfar) for side in range(2)]

    def meta(which, side, source, target):
        return pltpu.make_async_remote_copy(
            src_ref=source,
            dst_ref=target.at[side],
            send_sem=m_send.at[which, side],
            recv_sem=m_recv.at[which, side],
            device_id={"patch": away(-1 if side else 1)},
            device_id_type=MESH,
        )

    def half(ref, side):
        return ref.at[:, side * LANES : (side + 1) * LANES]

    meta1 = [meta(0, side, half(link1, side), rlink1) for side in range(2)]
    meta1 += [meta(1, side, half(weight1, side), rweight1) for side in range(2)]
    meta2 = [meta(2, side, link2, rlink2) for side in range(2)]
    meta2 += [meta(3, side, weight2, rweight2) for side in range(2)]

    outgoing = []

    def scatter(source, base):
        for piece in range(source.shape[1] // chunk):
            d = base // chunk + piece
            part = source.at[:, piece * chunk : (piece + 1) * chunk]
            copy = pltpu.make_async_remote_copy(
                src_ref=part,
                dst_ref=gathered.at[me],
                send_sem=g_send.at[d],
                recv_sem=g_recv.at[me],
                device_id={"lev": d},
                device_id_type=MESH,
            )
            outgoing.append((d, copy))

            @pl.when(me != d)
            def _():
                copy.start()

            @pl.when(me == d)
            def _():
                gathered[d] = part[...]

    def add_tail(into, n, tail, add):
        for c in range(0, n, wide):
            cols = slice(c, c + wide)
            got = product(ext, padded, n1, *tail, cols)
            old = into[:, cols]
            into[:, cols] = old + got if add else old - got

    lower = lax.broadcasted_iota(jnp.int32, (padded, LANES), 1) < halo2
    first = lax.broadcasted_iota(jnp.int32, (SUB, LANES), 1) < halo2

    def two(send):
        return jnp.concatenate([send[0, 1:2, :], send[0, 0:1, :]], axis=1)

    def side1(side):
        start = n1 + side * halo1
        return lambda link: (link >= start) & (link < start + halo1)

    def side2(same):
        def keep(link):
            ours = (link < n2 + halo2) == first
            return (link >= n2) & (ours if same else ~ours)

        return keep

    loaded(0, 1)
    pack(n1, cells)
    for side in range(2):
        picked(xs, n1, b1, sc1[0, 1 - side : 2 - side, :], asend.at[side])
    pl.semaphore_wait(barrier, 4 + n_lev - 1)
    for side in range(2):
        near1[side].start()
        far1[side].start()

    loaded(2, 5, 6, 13)
    put(ext, padded, 0, xs[:, n1:cells])
    pack(0, n1)
    for side in range(2):
        index = sd1[0, 1 - side : 2 - side, :]
        picked(pl1, 0, b1, index, half(link1, side))
        picked(pw1, 0, b1, index, half(weight1, side))
        picked(xs, 0, b1, index, fpart.at[side])

    def sent1(cols, got):
        for side in range(2):
            bsend[side] = fpart[side] - got[:, side * LANES : (side + 1) * LANES]

    stage(link1, weight1, merged, 0, 2 * LANES, b1, b1, ext, None, sent1)
    for copy in part1 + meta1:
        copy.start()

    def fine1(cols, got):
        det1[:, cols] = xs[:, cols] - got

    tail1 = (t1h, t1l)
    stage(pl1, pw1, merged, 0, n1, b1, e1 // LANES, ext, tail1, fine1)

    loaded(3, 4, 7, 8, 9, 10, 11, 12)
    picked(pl2, 0, b2, two(sd2), link2)
    picked(pw2, 0, b2, two(sd2), weight2)
    for copy in meta2:
        copy.start()

    for side in range(2):
        near1[side].wait_recv()
        put(ext, padded, n1 + side * halo1, arecv[side])
    add_tail(det1, n1, tail1, False)
    scatter(det1, 0)
    put(ext, padded, 0, det1[...])

    def coarse1(cols, got):
        at = pl.ds(pl.multiple_of(cols.start + n1, LANES), cols.size)
        sm1[:, cols] = xs[:, at] + got

    stage(ul1, uw1, merged, 0, n1, b1, e1 // LANES, ext, tail1, coarse1)
    for copy in meta1:
        copy.wait_recv()
    for side in range(2):
        early1[side] = reach(asend[1 - side], rlink1.at[side], rweight1.at[side], side1(1 - side))
    for side in range(2):
        far1[side].wait_recv()
        part1[side].wait_recv()
        value = brecv[side] - early1[side]
        value = value - reach(afar[side], rlink1.at[side], rweight1.at[side], side1(side))
        put(ext, padded, n1 + side * halo1, value)
    add_tail(sm1, n1, tail1, True)

    put(ext2, padded, 0, sm1[:, n2:n1])
    picked(sm1, n2, b2, two(sc2), own2)
    picked(sm1, 0, b2, two(sd2), fpart.at[0])

    def sent2(cols, got):
        part = pltpu.roll(fpart[0] - got, halo2, axis=1)
        csend[0] = jnp.where(lower, own2[...], part)
        csend[1] = jnp.where(lower, part, own2[...])

    stage(link2, weight2, merged, 0, LANES, b2, b2, ext2, None, sent2)
    for side in range(2):
        near2[side].start()
        far2[side].start()

    def fine2(cols, got):
        det2[:, cols] = sm1[:, cols] - got

    tail2 = (t2h, t2l)
    stage(pl2, pw2, merged, 0, n2, b2, e2 // LANES, ext2, tail2, fine2)
    scatter(det2, n1)

    prepare(ul2, uw2, merged, n2, e2 // LANES, (w2h, w2l))
    for copy in meta2:
        copy.wait_recv()
    turned = lax.broadcasted_iota(jnp.int32, (rlink2.shape[1], LANES), 1) < halo2
    link3[...] = jnp.where(turned, rlink2[0], rlink2[1])
    weight3[...] = jnp.where(turned, rweight2[0], rweight2[1])
    early2[...] = reach(own2[...], link3, weight3, side2(False))

    for side in range(2):
        near2[side].wait_recv()
    edge = jnp.where(lower, crecv[0], crecv[1])
    hsend[...] = edge

    forward = []
    for piece in range(n2 // chunk):
        d = n1 // chunk + piece
        copy = pltpu.make_async_remote_copy(
            src_ref=hsend,
            dst_ref=hrecv.at[me],
            send_sem=h_send.at[piece],
            recv_sem=h_recv.at[me],
            device_id={"lev": d},
            device_id_type=MESH,
        )
        forward.append((d, copy))

        @pl.when(me != d)
        def _():
            copy.start()

        @pl.when(me == d)
        def _():
            hrecv[d] = edge

    put(ext2, padded, n2, edge)
    for c in range(0, n2, wide):
        cols = slice(c, c + wide)
        value = det2[:, cols] - product(ext2, padded, n2, *tail2, cols)
        put(ext2, padded, c, value)

    for side in range(2):
        far2[side].wait_recv()
    value = pltpu.roll(jnp.where(lower, crecv[1], crecv[0]), halo2, axis=1) - early2[...]
    outer = jnp.where(lower, cfar[0], cfar[1])
    put(ext2, padded, n2, value - reach(outer, link3, weight3, side2(True)))
    for c in range(0, n2, wide):
        cols = slice(c, c + wide)
        sm2[:, cols] = sm1[:, n2 + c : n2 + c + wide] + product(ext2, padded, 0, w2h, w2l, cols)
    scatter(sm2, n1 + n2)

    for s in range(n_lev):

        @pl.when(me != s)
        def _():
            pltpu.make_async_remote_copy(
                src_ref=gathered.at[s],
                dst_ref=gathered.at[s],
                send_sem=g_send.at[s],
                recv_sem=g_recv.at[s],
                device_id={"lev": s},
                device_id_type=MESH,
            ).wait_recv()

    inner = (me >= n1 // chunk) & (me < (n1 + n2) // chunk)

    @pl.when(inner)
    def _():
        for s in range(n_lev):

            @pl.when(me != s)
            def _():
                pltpu.make_async_remote_copy(
                    src_ref=hrecv.at[s],
                    dst_ref=hrecv.at[s],
                    send_sem=h_send.at[0],
                    recv_sem=h_recv.at[s],
                    device_id={"lev": s},
                    device_id_type=MESH,
                ).wait_recv()

        at = pl.multiple_of((me - n1 // chunk) * chunk, LANES)
        cols = pl.ds(at, chunk)
        for s in range(n_lev):
            high, low = halves(hrecv[s])
            both = jnp.concatenate([high, low], axis=0)
            both = jnp.dot(both, t2h[:, cols], preferred_element_type=jnp.float32)
            rest = jnp.dot(high, t2l[:, cols], preferred_element_type=jnp.float32)
            gathered[s] = gathered[s] - (both[0:padded] + both[padded : 2 * padded] + rest)

    for group in (near1, far1, part1, near2, far2, meta1, meta2):
        for copy in group:
            copy.wait_send()
    for d, copy in outgoing + forward:

        @pl.when(me != d)
        def _():
            copy.wait_send()


def transform(gathered, t_high, t_low, out):
    groups, padded, chunk = gathered.shape
    tracers, levels, _ = out.shape
    high, low = halves(gathered[...].reshape(groups * padded, chunk))
    for t in range(tracers):
        rows = slice(t * levels, (t + 1) * levels)
        out[t] = (
            jnp.dot(t_high[rows, :], high, preferred_element_type=jnp.float32)
            + jnp.dot(t_high[rows, :], low, preferred_element_type=jnp.float32)
            + jnp.dot(t_low[rows, :], high, preferred_element_type=jnp.float32)
        )


def on_device(n_patch, n_lev, *args):
    field, sc1 = args[0], args[1]
    own, tracers, cells = field.shape
    levels = own * n_lev
    rows = own * tracers
    padded = -(-rows // (2 * SUB)) * (2 * SUB)
    n1, n2 = cells // 2, cells // 4
    e1 = n1 + 2 * sc1.shape[2]
    e2 = n2 + 2 * args[3].shape[2]
    chunk = cells // n_lev
    slots = args[5].shape[0]
    t_high, t_low = spread_table(levels, tracers, n_lev, padded)
    f32, bf16 = jnp.float32, jnp.bfloat16
    gathered = pl.pallas_call(
        functools.partial(body, n_patch, n_lev, levels),
        out_shape=jax.ShapeDtypeStruct((n_lev, padded, chunk), f32),
        in_specs=[pl.BlockSpec(memory_space=pltpu.HBM)] * 13,
        out_specs=pl.BlockSpec(memory_space=pltpu.VMEM),
        scratch_shapes=[
            pltpu.VMEM((tracers, own, cells), f32),
            *(pltpu.VMEM(a.shape, a.dtype) for a in args[1:]),
            pltpu.VMEM((padded, cells), f32),
            pltpu.VMEM((2 * padded, e1), bf16),
            pltpu.VMEM((2 * padded, e2), bf16),
            pltpu.VMEM((2, slots, -(-(e1 // LANES) // SUB) * SUB, LANES), f32),
            *[pltpu.VMEM((e1 - n1, n1), bf16)] * 2,
            *[pltpu.VMEM((e2 - n2, n2), bf16)] * 2,
            *[pltpu.VMEM((e2, n2), bf16)] * 2,
            *[pltpu.VMEM((padded, n1), f32)] * 2,
            *[pltpu.VMEM((padded, n2), f32)] * 2,
            *[pltpu.VMEM((2, padded, LANES), f32)] * 8,
            pltpu.VMEM((slots, 2 * LANES), jnp.int32),
            pltpu.VMEM((slots, 2 * LANES), f32),
            pltpu.VMEM((slots, LANES), jnp.int32),
            pltpu.VMEM((slots, LANES), f32),
            pltpu.VMEM((slots, LANES), jnp.int32),
            pltpu.VMEM((slots, LANES), f32),
            pltpu.VMEM((2, slots, LANES), jnp.int32),
            pltpu.VMEM((2, slots, LANES), f32),
            pltpu.VMEM((2, slots, LANES), jnp.int32),
            pltpu.VMEM((2, slots, LANES), f32),
            pltpu.VMEM((2, padded, LANES), f32),
            pltpu.VMEM((padded, LANES), f32),
            pltpu.VMEM((2, padded, LANES), f32),
            pltpu.VMEM((padded, LANES), f32),
            pltpu.VMEM((padded, LANES), f32),
            pltpu.VMEM((n_lev, padded, LANES), f32),
            pltpu.SemaphoreType.DMA((14,)),
            pltpu.SemaphoreType.DMA((5, 2)),
            pltpu.SemaphoreType.DMA((5, 2)),
            pltpu.SemaphoreType.DMA((4, 2)),
            pltpu.SemaphoreType.DMA((4, 2)),
            pltpu.SemaphoreType.DMA((n_lev,)),
            pltpu.SemaphoreType.DMA((n_lev,)),
            pltpu.SemaphoreType.DMA((n2 // chunk,)),
            pltpu.SemaphoreType.DMA((n_lev,)),
        ],
        compiler_params=pltpu.CompilerParams(
            collective_id=0, has_side_effects=True, vmem_limit_bytes=16 << 20
        ),
    )(*(pltpu.with_memory_space_constraint(a, pltpu.HBM) for a in (jnp.transpose(field, (1, 0, 2)), *args[1:])))
    result = pl.pallas_call(
        transform,
        out_shape=jax.ShapeDtypeStruct((tracers, levels, chunk), f32),
        in_specs=[pl.BlockSpec(memory_space=pltpu.VMEM)] * 3,
        out_specs=pl.BlockSpec(memory_space=pltpu.VMEM),
        compiler_params=pltpu.CompilerParams(vmem_limit_bytes=8 << 20),
    )(gathered, jnp.asarray(t_high), jnp.asarray(t_low))
    return jnp.transpose(result, (1, 0, 2))


def solution(mesh):
    in_specs = (P("lev", None, "patch"),)
    in_specs += (P("patch", None, None),) * 4
    in_specs += (P(None, "patch"),) * 8
    out_specs = P(None, None, ("patch", "lev"))
    fn = functools.partial(on_device, mesh.shape["patch"], mesh.shape["lev"])
    return jax.shard_map(
        fn, mesh=mesh, in_specs=in_specs, out_specs=out_specs, check_vma=False
    )
```

```python
import functools

import jax
import jax.numpy as jnp
import ml_dtypes
import numpy as np
from jax import lax
from jax.experimental import pallas as pl
from jax.experimental.pallas import tpu as pltpu
from jax.sharding import PartitionSpec as P

LANES = 128
SUB = 8
MESH = pl.DeviceIdType.MESH


def cosine_table(length):
    rows = np.arange(length, dtype=np.float64)[:, None]
    columns = np.arange(length, dtype=np.float64)[None, :]
    matrix = np.cos(np.pi * (columns + 0.5) * rows / length) * np.sqrt(2.0 / length)
    matrix[0] *= np.sqrt(0.5)
    return matrix


def spread_table(levels, tracers, groups, padded):
    own = levels // groups
    table = cosine_table(levels).reshape(levels, groups, own)
    wide = np.zeros((tracers, levels, groups, padded))
    for t in range(tracers):
        wide[t, :, :, t * own : (t + 1) * own] = table
    wide = wide.reshape(levels * tracers, groups * padded).astype(np.float32)
    high = wide.astype(ml_dtypes.bfloat16)
    low = (wide - high.astype(np.float32)).astype(ml_dtypes.bfloat16)
    return high, low


def halves(x):
    high = x.astype(jnp.bfloat16)
    low = (x - high.astype(jnp.float32)).astype(jnp.bfloat16)
    return high, low


def along(table, index):
    numbers = lax.GatherDimensionNumbers(
        offset_dims=(),
        collapsed_slice_dims=(0,),
        start_index_map=(0,),
        operand_batching_dims=(1,),
        start_indices_batching_dims=(1,),
    )
    mode = lax.GatherScatterMode.PROMISE_IN_BOUNDS
    return lax.gather(table, index[:, :, None], numbers, (1, 1), mode=mode)


def tile(links, weights, merged, cols, blocks):
    slots = links.shape[0]
    lane = []
    block = []
    weight = []
    for k in range(slots):
        link = jnp.broadcast_to(links[k : k + 1, cols], (SUB, LANES))
        lane.append(link & (LANES - 1))
        block.append(link >> 7)
        weight.append(jnp.broadcast_to(weights[k : k + 1, cols], (SUB, LANES)))
    room = merged.shape[0] // slots
    which = lax.broadcasted_iota(jnp.int32, (SUB, LANES), 0)
    same = [[lane[j] == lane[k] for j in range(k)] for k in range(slots)]
    for g in range(-(-blocks // SUB)):
        placed = []
        for k in range(slots):
            mine = jnp.where(block[k] == which + g * SUB, weight[k], 0.0)
            total = mine
            for j in range(k):
                total = total + jnp.where(same[k][j], placed[j], 0.0)
            placed.append(mine)
            at = k * room + g * SUB
            merged[at : at + SUB, :] = total
    none = jnp.zeros((2 * SUB - slots, LANES), jnp.float32)
    tables = []
    for b in range(blocks):
        row = merged[pl.ds(b, slots, stride=room), :]
        tables.append(halves(jnp.concatenate([row, none], axis=0)))
    short = [jnp.concatenate([v, v], axis=0).astype(jnp.int16) for v in lane]
    strips = []
    for s in range(LANES // (2 * SUB)):
        rows = lax.broadcasted_iota(jnp.int16, (2 * SUB, LANES), 0) + jnp.int16(s * 2 * SUB)
        index = jnp.full((2 * SUB, LANES), slots, jnp.int16)
        for k in range(slots):
            index = jnp.where(short[k] == rows, jnp.int16(k), index)
        strips.append(index)
    return tables, strips


def spread(tiles, part, first, last):
    return jnp.concatenate(
        [
            jnp.concatenate(
                [along(tables[b][part], index) for b in range(first, last) for index in strips],
                axis=0,
            )
            for tables, strips in tiles
        ],
        axis=1,
    )


def stage(links, weights, merged, first, count, own, blocks, ext, tail, emit):
    padded = ext.shape[0] // 2
    depth = own * LANES
    width = min(count, 2 * LANES)

    def step(t, _):
        start = pl.multiple_of(first + t * width, width)
        tiles = [
            tile(
                links, weights, merged.at[h],
                pl.ds(pl.multiple_of(start + h * LANES, LANES), LANES), blocks,
            )
            for h in range(width // LANES)
        ]
        high = spread(tiles, 0, 0, own)
        low = spread(tiles, 1, 0, own)
        both = jnp.dot(ext[:, 0:depth], high, preferred_element_type=jnp.float32)
        rest = jnp.dot(ext[0:padded, 0:depth], low, preferred_element_type=jnp.float32)
        cols = pl.ds(start, width)
        emit(cols, both[0:padded] + both[padded : 2 * padded] + rest)
        if tail is not None:
            tail[0][:, cols] = spread(tiles, 0, own, blocks)
            tail[1][:, cols] = spread(tiles, 1, own, blocks)
        return 0

    lax.fori_loop(0, count // width, step, 0, unroll=2 if count > width else 1)


def prepare(links, weights, merged, count, blocks, out):
    def step(t, _):
        cols = pl.ds(pl.multiple_of(t * LANES, LANES), LANES)
        tiles = [tile(links, weights, merged.at[0], cols, blocks)]
        out[0][:, cols] = spread(tiles, 0, 0, blocks)
        out[1][:, cols] = spread(tiles, 1, 0, blocks)
        return 0

    lax.fori_loop(0, count // LANES, step, 0)


def picked(source, start, blocks, index, out):
    lane = jnp.broadcast_to(index & (LANES - 1), (SUB, LANES))
    block = jnp.broadcast_to(index >> 7, (SUB, LANES))
    for r in range(source.shape[0] // SUB):
        rows = slice(r * SUB, (r + 1) * SUB)
        got = None
        for b in range(blocks):
            cols = slice(start + b * LANES, start + (b + 1) * LANES)
            t = jnp.take_along_axis(source[rows, cols], lane, axis=1)
            got = t if got is None else jnp.where(block == b, t, got)
        out[rows, :] = got


def put(ext, padded, at, value):
    high, low = halves(value)
    width = value.shape[1]
    ext[0:padded, at : at + width] = high
    ext[padded : 2 * padded, at : at + width] = low


def product(ext, padded, start, w_high, w_low, cols):
    k = slice(start, start + w_high.shape[0])
    both = jnp.dot(ext[:, k], w_high[:, cols], preferred_element_type=jnp.float32)
    rest = jnp.dot(ext[0:padded, k], w_low[:, cols], preferred_element_type=jnp.float32)
    return both[0:padded] + both[padded : 2 * padded] + rest


def reach(value, links, weights, keep):
    padded = value.shape[0]
    rows = [value[r * SUB : (r + 1) * SUB, :] for r in range(padded // SUB)]
    totals = [None] * len(rows)
    for k in range(links.shape[0]):
        link = jnp.broadcast_to(links[k : k + 1, :], (SUB, LANES))
        weight = jnp.broadcast_to(weights[k : k + 1, :], (SUB, LANES))
        weight = jnp.where(keep(link), weight, 0.0)
        lane = link & (LANES - 1)
        for r, row in enumerate(rows):
            term = weight * jnp.take_along_axis(row, lane, axis=1)
            totals[r] = term if totals[r] is None else totals[r] + term
    return jnp.concatenate(totals, axis=0)


def body(n_patch, n_lev, levels, *refs):
    given, gathered, held, rest = refs[:13], refs[13], refs[14:27], refs[27:]
    field, sc1, sd1, sc2, sd2, pl1, pw1, ul1, uw1, pl2, pw2, ul2, uw2 = held
    (
        xs, ext, ext2, merged, t1h, t1l, w1h, w1l, w3h, w3l, w4h, w4l, p2h, p2l, w2h, w2l, qh, ql,
        det1, sm1, det2, sm2,
        asend, arecv, afar, bsend, brecv, csend, crecv, cfar,
        link1, weight1, link2, weight2, link3, weight3, link4, weight4, rlink1, rweight1, rlink2, rweight2,
        fpart, own2, early1, hsend, hrecv,
        in_sem, x_send, x_recv, m_send, m_recv, g_send, g_recv, h_send, h_recv,
    ) = rest
    tracers, own, cells = field.shape
    rows = own * tracers
    padded = xs.shape[0]
    n1 = cells // 2
    n2 = cells // 4
    halo1 = sc1.shape[2]
    halo2 = sc2.shape[2]
    chunk = cells // n_lev
    b1 = n1 // LANES
    b2 = n2 // LANES
    e1 = n1 + 2 * halo1
    e2 = n2 + 2 * halo2
    wide = 256
    me = lax.axis_index("lev")
    patch = lax.axis_index("patch")

    def away(steps):
        return lax.rem(patch + n_patch + steps, n_patch)

    barrier = pltpu.get_barrier_semaphore()
    for steps in (-2, -1, 1, 2):
        pl.semaphore_signal(barrier, inc=1, device_id={"patch": away(steps)}, device_id_type=MESH)
    for d in range(1, n_lev):
        pl.semaphore_signal(
            barrier, inc=1, device_id={"lev": lax.rem(me + d, n_lev)}, device_id_type=MESH
        )

    coarse = (slice(None), slice(None), slice(n1, cells))
    fine = (slice(None), slice(None), slice(0, n1))
    loads = {0: pltpu.make_async_copy(given[0].at[coarse], field.at[coarse], in_sem.at[0])}
    for i in (1, 5, 6, 2):
        loads[i] = pltpu.make_async_copy(given[i], held[i], in_sem.at[i])
    loads[13] = pltpu.make_async_copy(given[0].at[fine], field.at[fine], in_sem.at[13])
    for i in (3, 4, 7, 8, 9, 10, 11, 12):
        loads[i] = pltpu.make_async_copy(given[i], held[i], in_sem.at[i])
    for load in loads.values():
        load.start()

    def loaded(*which):
        for i in which:
            loads[i].wait()

    def pack(start, stop):
        if padded > rows:
            edge = rows // SUB * SUB
            xs[edge:padded, start:stop] = jnp.zeros((padded - edge, stop - start), jnp.float32)
        for t in range(tracers):
            xs[t * own : (t + 1) * own, start:stop] = field[t, :, start:stop]

    def message(which, side, steps, source, target):
        return pltpu.make_async_remote_copy(
            src_ref=source.at[side],
            dst_ref=target.at[side],
            send_sem=x_send.at[which, side],
            recv_sem=x_recv.at[which, side],
            device_id={"patch": away(-steps if side else steps)},
            device_id_type=MESH,
        )

    near1 = [message(0, side, 1, asend, arecv) for side in range(2)]
    far1 = [message(1, side, 2, asend, afar) for side in range(2)]
    part1 = [message(2, side, 1, bsend, brecv) for side in range(2)]
    near2 = [message(3, side, 1, csend, crecv) for side in range(2)]
    far2 = [message(4, side, 2, csend, cfar) for side in range(2)]

    def meta(which, side, source, target):
        return pltpu.make_async_remote_copy(
            src_ref=source,
            dst_ref=target.at[side],
            send_sem=m_send.at[which, side],
            recv_sem=m_recv.at[which, side],
            device_id={"patch": away(-1 if side else 1)},
            device_id_type=MESH,
        )

    def half(ref, side):
        return ref.at[:, side * LANES : (side + 1) * LANES]

    meta1 = [meta(0, side, half(link1, side), rlink1) for side in range(2)]
    meta1 += [meta(1, side, half(weight1, side), rweight1) for side in range(2)]
    meta2 = [meta(2, side, link2, rlink2) for side in range(2)]
    meta2 += [meta(3, side, weight2, rweight2) for side in range(2)]

    outgoing = []

    def scatter(source, base):
        for piece in range(source.shape[1] // chunk):
            d = base // chunk + piece
            part = source.at[:, piece * chunk : (piece + 1) * chunk]
            copy = pltpu.make_async_remote_copy(
                src_ref=part,
                dst_ref=gathered.at[me],
                send_sem=g_send.at[d],
                recv_sem=g_recv.at[me],
                device_id={"lev": d},
                device_id_type=MESH,
            )
            outgoing.append((d, copy))

            @pl.when(me != d)
            def _():
                copy.start()

            @pl.when(me == d)
            def _():
                gathered[d] = part[...]

    lower = lax.broadcasted_iota(jnp.int32, (padded, LANES), 1) < halo2
    first = lax.broadcasted_iota(jnp.int32, (SUB, LANES), 1) < halo2

    def two(send):
        return jnp.concatenate([send[0, 1:2, :], send[0, 0:1, :]], axis=1)

    def side1(side):
        start = n1 + side * halo1
        return lambda link: (link >= start) & (link < start + halo1)

    def side2(same):
        def keep(link):
            ours = (link < n2 + halo2) == first
            return (link >= n2) & (ours if same else ~ours)

        return keep

    loaded(0, 1)
    pack(n1, cells)
    for side in range(2):
        picked(xs, n1, b1, sc1[0, 1 - side : 2 - side, :], asend.at[side])
    put(ext, padded, 0, xs[:, n1:cells])
    loaded(2, 5, 6, 13, 3, 4, 7, 8, 9, 10, 11, 12)
    pack(0, n1)

    def fine1(cols, got):
        det1[:, cols] = xs[:, cols] - got

    def detail():
        stage(pl1, pw1, merged, 0, n1, b1, e1 // LANES, ext, (t1h, t1l), fine1)

    def level2():
        prepare(link2, weight2, merged, LANES, b2, (w4h, w4l))
        prepare(pl2, pw2, merged, n2, e2 // LANES, (p2h, p2l))
        prepare(ul2, uw2, merged, n2, e2 // LANES, (w2h, w2l))

    for side in range(2):
        index = sd1[0, 1 - side : 2 - side, :]
        picked(pl1, 0, b1, index, half(link1, side))
        picked(pw1, 0, b1, index, half(weight1, side))
    picked(pl2, 0, b2, two(sd2), link2)
    picked(pw2, 0, b2, two(sd2), weight2)
    picked(ul1, 0, b2, two(sd2), link4)
    picked(uw1, 0, b2, two(sd2), weight4)

    @pl.when(patch < 2)
    def _():
        detail()
        level2()

    pl.semaphore_wait(barrier, 4 + n_lev - 1)
    for copy in near1 + far1 + meta1 + meta2:
        copy.start()

    @pl.when(patch >= 2)
    def _():
        detail()

    for side in range(2):
        picked(det1, 0, b1, sd1[0, 1 - side : 2 - side, :], bsend.at[side])
    for copy in part1:
        copy.start()
    picked(xs, n1, b2, two(sd2), fpart.at[0])
    prepare(ul1, uw1, merged, n1, e1 // LANES, (w1h, w1l))
    prepare(link4, weight4, merged, LANES, e1 // LANES, (w3h, w3l))

    @pl.when(patch >= 2)
    def _():
        level2()

    for side in range(2):
        near1[side].wait_recv()
        put(ext, padded, n1 + side * halo1, arecv[side])
    for c in range(0, n1, wide):
        cols = slice(c, c + wide)
        det1[:, cols] = det1[:, cols] - product(ext, padded, n1, t1h, t1l, cols)
    scatter(det1, 0)
    put(ext, padded, 0, det1[...])
    for copy in meta1 + far1:
        copy.wait_recv()
    for side in range(2):
        known = reach(asend[1 - side], rlink1.at[side], rweight1.at[side], side1(1 - side))
        outer = reach(afar[side], rlink1.at[side], rweight1.at[side], side1(side))
        early1[side] = known + outer
    for side in range(2):
        part1[side].wait_recv()
        put(ext, padded, n1 + side * halo1, brecv[side] - early1[side])

    def smooth(start, stop):
        for c in range(start, stop, wide):
            cols = slice(c, c + wide)
            sm1[:, cols] = xs[:, n1 + c : n1 + c + wide] + product(ext, padded, 0, w1h, w1l, cols)

    smooth(n2, n1)
    put(ext2, padded, 0, sm1[:, n2:n1])
    picked(sm1, n2, b2, two(sc2), own2)
    every_lane = slice(0, LANES)
    part = fpart[0] + product(ext, padded, 0, w3h, w3l, every_lane)
    part = part - product(ext2, padded, 0, w4h, w4l, every_lane)
    part = pltpu.roll(part, halo2, axis=1)
    csend[0] = jnp.where(lower, own2[...], part)
    csend[1] = jnp.where(lower, part, own2[...])
    for copy in near2 + far2:
        copy.start()

    smooth(0, n2)
    own_rows = slice(0, n2)
    for c in range(0, n2, wide):
        cols = slice(c, c + wide)
        got = product(ext2, padded, 0, p2h.at[own_rows], p2l.at[own_rows], cols)
        det2[:, cols] = sm1[:, cols] - got
    scatter(det2, n1)
    put(ext2, padded, 0, det2[...])
    for copy in meta2:
        copy.wait_recv()
    turned = lax.broadcasted_iota(jnp.int32, (rlink2.shape[1], LANES), 1) < halo2
    link3[...] = jnp.where(turned, rlink2[0], rlink2[1])
    weight3[...] = jnp.where(turned, rweight2[0], rweight2[1])
    put(ext2, padded, n2, -reach(own2[...], link3, weight3, side2(False)))

    for c in range(0, n2, wide):
        cols = slice(c, c + wide)
        sm2[:, cols] = sm1[:, n2 + c : n2 + c + wide] + product(ext2, padded, 0, w2h, w2l, cols)
    scatter(sm2, n1 + n2)

    @pl.when(me >= (n1 + n2) // chunk)
    def _():
        for c in range(0, n2, wide):
            cols = slice(c, c + wide)
            both = jnp.concatenate([p2h[n2:e2, :], p2l[n2:e2, :]], axis=0)
            both = jnp.dot(both, w2h[own_rows, cols], preferred_element_type=jnp.float32)
            rest = jnp.dot(p2h[n2:e2, :], w2l[own_rows, cols], preferred_element_type=jnp.float32)
            high, low = halves(-(both[0:LANES] + both[LANES : 2 * LANES] + rest))
            qh[0:LANES, cols] = high
            ql[0:LANES, cols] = low
            qh[LANES : 2 * LANES, cols] = w2h[n2:e2, cols]
            ql[LANES : 2 * LANES, cols] = w2l[n2:e2, cols]

    for copy in near2 + far2:
        copy.wait_recv()
    hsend[0] = jnp.where(lower, crecv[0], crecv[1])
    value = pltpu.roll(jnp.where(lower, crecv[1], crecv[0]), halo2, axis=1)
    outer = jnp.where(lower, cfar[0], cfar[1])
    hsend[1] = value - reach(outer, link3, weight3, side2(True))

    forward = []
    for piece in range(2 * n2 // chunk):
        d = n1 // chunk + piece
        count = 1 if piece < n2 // chunk else 2
        copy = pltpu.make_async_remote_copy(
            src_ref=hsend.at[0:count],
            dst_ref=hrecv.at[me, 0:count],
            send_sem=h_send.at[piece],
            recv_sem=h_recv.at[me],
            device_id={"lev": d},
            device_id_type=MESH,
        )
        forward.append((d, copy))

        @pl.when(me != d)
        def _():
            copy.start()

        @pl.when(me == d)
        def _():
            hrecv[d, 0:count] = hsend[0:count]

    for s in range(n_lev):

        @pl.when(me != s)
        def _():
            pltpu.make_async_remote_copy(
                src_ref=gathered.at[s],
                dst_ref=gathered.at[s],
                send_sem=g_send.at[s],
                recv_sem=g_recv.at[s],
                device_id={"lev": s},
                device_id_type=MESH,
            ).wait_recv()

    def arrived(count):
        for s in range(n_lev):

            @pl.when(me != s)
            def _():
                pltpu.make_async_remote_copy(
                    src_ref=hrecv.at[s, 0:count],
                    dst_ref=hrecv.at[s, 0:count],
                    send_sem=h_send.at[0],
                    recv_sem=h_recv.at[s],
                    device_id={"lev": s},
                    device_id_type=MESH,
                ).wait_recv()

    def times(value, high, low):
        top, rest = halves(value)
        count = value.shape[0]
        both = jnp.concatenate([top, rest], axis=0)
        both = jnp.dot(both, high, preferred_element_type=jnp.float32)
        rest = jnp.dot(top, low, preferred_element_type=jnp.float32)
        return both[0:count] + both[count : 2 * count] + rest

    def every(which):
        return jnp.concatenate([hrecv[s, which] for s in range(n_lev)], axis=0)

    @pl.when((me >= n1 // chunk) & (me < (n1 + n2) // chunk))
    def _():
        arrived(1)
        cols = pl.ds(pl.multiple_of((me - n1 // chunk) * chunk, LANES), chunk)
        change = times(every(0), p2h[n2:e2, cols], p2l[n2:e2, cols])
        for s in range(n_lev):
            gathered[s] = gathered[s] - change[s * padded : (s + 1) * padded]

    @pl.when(me >= (n1 + n2) // chunk)
    def _():
        arrived(2)
        cols = pl.ds(pl.multiple_of((me - (n1 + n2) // chunk) * chunk, LANES), chunk)
        change = times(jnp.concatenate([every(0), every(1)], axis=1), qh[:, cols], ql[:, cols])
        for s in range(n_lev):
            gathered[s] = gathered[s] + change[s * padded : (s + 1) * padded]

    for group in (near1, far1, part1, near2, far2, meta1, meta2):
        for copy in group:
            copy.wait_send()
    for d, copy in outgoing + forward:

        @pl.when(me != d)
        def _():
            copy.wait_send()


def transform(gathered, t_high, t_low, out):
    groups, padded, chunk = gathered.shape
    tracers, levels, _ = out.shape
    high, low = halves(gathered[...].reshape(groups * padded, chunk))
    for t in range(tracers):
        rows = slice(t * levels, (t + 1) * levels)
        out[t] = (
            jnp.dot(t_high[rows, :], high, preferred_element_type=jnp.float32)
            + jnp.dot(t_high[rows, :], low, preferred_element_type=jnp.float32)
            + jnp.dot(t_low[rows, :], high, preferred_element_type=jnp.float32)
        )


def on_device(n_patch, n_lev, *args):
    field, sc1 = args[0], args[1]
    own, tracers, cells = field.shape
    levels = own * n_lev
    rows = own * tracers
    padded = -(-rows // (2 * SUB)) * (2 * SUB)
    n1, n2 = cells // 2, cells // 4
    e1 = n1 + 2 * sc1.shape[2]
    e2 = n2 + 2 * args[3].shape[2]
    chunk = cells // n_lev
    slots = args[5].shape[0]
    t_high, t_low = spread_table(levels, tracers, n_lev, padded)
    f32, bf16 = jnp.float32, jnp.bfloat16
    gathered = pl.pallas_call(
        functools.partial(body, n_patch, n_lev, levels),
        out_shape=jax.ShapeDtypeStruct((n_lev, padded, chunk), f32),
        in_specs=[pl.BlockSpec(memory_space=pltpu.HBM)] * 13,
        out_specs=pl.BlockSpec(memory_space=pltpu.VMEM),
        scratch_shapes=[
            pltpu.VMEM((tracers, own, cells), f32),
            *(pltpu.VMEM(a.shape, a.dtype) for a in args[1:]),
            pltpu.VMEM((padded, cells), f32),
            pltpu.VMEM((2 * padded, e1), bf16),
            pltpu.VMEM((2 * padded, e2), bf16),
            pltpu.VMEM((2, slots * -(-(e1 // LANES) // SUB) * SUB, LANES), f32),
            *[pltpu.VMEM((e1 - n1, n1), bf16)] * 2,
            *[pltpu.VMEM((e1, n1), bf16)] * 2,
            *[pltpu.VMEM((e1, LANES), bf16)] * 2,
            *[pltpu.VMEM((n2, LANES), bf16)] * 2,
            *[pltpu.VMEM((e2, n2), bf16)] * 4,
            *[pltpu.VMEM((2 * (e2 - n2), n2), bf16)] * 2,
            *[pltpu.VMEM((padded, n1), f32)] * 2,
            *[pltpu.VMEM((padded, n2), f32)] * 2,
            *[pltpu.VMEM((2, padded, LANES), f32)] * 8,
            pltpu.VMEM((slots, 2 * LANES), jnp.int32),
            pltpu.VMEM((slots, 2 * LANES), f32),
            pltpu.VMEM((slots, LANES), jnp.int32),
            pltpu.VMEM((slots, LANES), f32),
            pltpu.VMEM((slots, LANES), jnp.int32),
            pltpu.VMEM((slots, LANES), f32),
            pltpu.VMEM((slots, LANES), jnp.int32),
            pltpu.VMEM((slots, LANES), f32),
            pltpu.VMEM((2, slots, LANES), jnp.int32),
            pltpu.VMEM((2, slots, LANES), f32),
            pltpu.VMEM((2, slots, LANES), jnp.int32),
            pltpu.VMEM((2, slots, LANES), f32),
            pltpu.VMEM((2, padded, LANES), f32),
            pltpu.VMEM((padded, LANES), f32),
            pltpu.VMEM((2, padded, LANES), f32),
            pltpu.VMEM((2, padded, LANES), f32),
            pltpu.VMEM((n_lev, 2, padded, LANES), f32),
            pltpu.SemaphoreType.DMA((14,)),
            pltpu.SemaphoreType.DMA((5, 2)),
            pltpu.SemaphoreType.DMA((5, 2)),
            pltpu.SemaphoreType.DMA((4, 2)),
            pltpu.SemaphoreType.DMA((4, 2)),
            pltpu.SemaphoreType.DMA((n_lev,)),
            pltpu.SemaphoreType.DMA((n_lev,)),
            pltpu.SemaphoreType.DMA((2 * n2 // chunk,)),
            pltpu.SemaphoreType.DMA((n_lev,)),
        ],
        compiler_params=pltpu.CompilerParams(
            collective_id=0, has_side_effects=True, vmem_limit_bytes=24 << 20
        ),
    )(*(pltpu.with_memory_space_constraint(a, pltpu.HBM) for a in (jnp.transpose(field, (1, 0, 2)), *args[1:])))
    result = pl.pallas_call(
        transform,
        out_shape=jax.ShapeDtypeStruct((tracers, levels, chunk), f32),
        in_specs=[pl.BlockSpec(memory_space=pltpu.VMEM)] * 3,
        out_specs=pl.BlockSpec(memory_space=pltpu.VMEM),
        compiler_params=pltpu.CompilerParams(vmem_limit_bytes=8 << 20),
    )(gathered, jnp.asarray(t_high), jnp.asarray(t_low))
    return jnp.transpose(result, (1, 0, 2))


def solution(mesh):
    in_specs = (P("lev", None, "patch"),)
    in_specs += (P("patch", None, None),) * 4
    in_specs += (P(None, "patch"),) * 8
    out_specs = P(None, None, ("patch", "lev"))
    fn = functools.partial(on_device, mesh.shape["patch"], mesh.shape["lev"])
    return jax.shard_map(
        fn, mesh=mesh, in_specs=in_specs, out_specs=out_specs, check_vma=False
    )
```

```python
import functools

import jax
import jax.numpy as jnp
import ml_dtypes
import numpy as np
from jax import lax
from jax.experimental import pallas as pl
from jax.experimental.pallas import tpu as pltpu
from jax.sharding import PartitionSpec as P

LANES = 128
SUB = 8
MESH = pl.DeviceIdType.MESH


def cosine_table(length):
    rows = np.arange(length, dtype=np.float64)[:, None]
    columns = np.arange(length, dtype=np.float64)[None, :]
    matrix = np.cos(np.pi * (columns + 0.5) * rows / length) * np.sqrt(2.0 / length)
    matrix[0] *= np.sqrt(0.5)
    return matrix


def spread_table(levels, tracers, groups, padded):
    own = levels // groups
    table = cosine_table(levels).reshape(levels, groups, own)
    wide = np.zeros((tracers, levels, groups, padded))
    for t in range(tracers):
        wide[t, :, :, t * own : (t + 1) * own] = table
    wide = wide.reshape(levels * tracers, groups * padded).astype(np.float32)
    high = wide.astype(ml_dtypes.bfloat16)
    low = (wide - high.astype(np.float32)).astype(ml_dtypes.bfloat16)
    return high, low


def halves(x):
    high = x.astype(jnp.bfloat16)
    low = (x - high.astype(jnp.float32)).astype(jnp.bfloat16)
    return high, low


def along(table, index):
    numbers = lax.GatherDimensionNumbers(
        offset_dims=(),
        collapsed_slice_dims=(0,),
        start_index_map=(0,),
        operand_batching_dims=(1,),
        start_indices_batching_dims=(1,),
    )
    mode = lax.GatherScatterMode.PROMISE_IN_BOUNDS
    return lax.gather(table, index[:, :, None], numbers, (1, 1), mode=mode)


def tile(links, weights, merged, cols, blocks):
    slots = links.shape[0]
    lane = []
    block = []
    weight = []
    for k in range(slots):
        link = jnp.broadcast_to(links[k : k + 1, cols], (SUB, LANES))
        lane.append(link & (LANES - 1))
        block.append(link >> 7)
        weight.append(jnp.broadcast_to(weights[k : k + 1, cols], (SUB, LANES)))
    room = merged.shape[0] // slots
    which = lax.broadcasted_iota(jnp.int32, (SUB, LANES), 0)
    same = [[lane[j] == lane[k] for j in range(k)] for k in range(slots)]
    for g in range(-(-blocks // SUB)):
        placed = []
        for k in range(slots):
            mine = jnp.where(block[k] == which + g * SUB, weight[k], 0.0)
            total = mine
            for j in range(k):
                total = total + jnp.where(same[k][j], placed[j], 0.0)
            placed.append(mine)
            at = k * room + g * SUB
            merged[at : at + SUB, :] = total
    none = jnp.zeros((2 * SUB - slots, LANES), jnp.float32)
    tables = []
    for b in range(blocks):
        row = merged[pl.ds(b, slots, stride=room), :]
        tables.append(halves(jnp.concatenate([row, none], axis=0)))
    short = [jnp.concatenate([v, v], axis=0).astype(jnp.int16) for v in lane]
    strips = []
    for s in range(LANES // (2 * SUB)):
        rows = lax.broadcasted_iota(jnp.int16, (2 * SUB, LANES), 0) + jnp.int16(s * 2 * SUB)
        index = jnp.full((2 * SUB, LANES), slots, jnp.int16)
        for k in range(slots):
            index = jnp.where(short[k] == rows, jnp.int16(k), index)
        strips.append(index)
    return tables, strips


def spread(tiles, part, first, last):
    return jnp.concatenate(
        [
            jnp.concatenate(
                [along(tables[b][part], index) for b in range(first, last) for index in strips],
                axis=0,
            )
            for tables, strips in tiles
        ],
        axis=1,
    )


def stage(links, weights, merged, first, count, own, blocks, ext, tail, emit):
    padded = ext.shape[0] // 2
    depth = own * LANES
    width = min(count, 2 * LANES)

    def step(t, _):
        start = pl.multiple_of(first + t * width, width)
        tiles = [
            tile(
                links, weights, merged.at[h],
                pl.ds(pl.multiple_of(start + h * LANES, LANES), LANES), blocks,
            )
            for h in range(width // LANES)
        ]
        high = spread(tiles, 0, 0, own)
        low = spread(tiles, 1, 0, own)
        both = jnp.dot(ext[:, 0:depth], high, preferred_element_type=jnp.float32)
        rest = jnp.dot(ext[0:padded, 0:depth], low, preferred_element_type=jnp.float32)
        cols = pl.ds(start, width)
        emit(cols, both[0:padded] + both[padded : 2 * padded] + rest)
        if tail is not None:
            tail[0][:, cols] = spread(tiles, 0, own, blocks)
            tail[1][:, cols] = spread(tiles, 1, own, blocks)
        return 0

    lax.fori_loop(0, count // width, step, 0, unroll=2 if count > width else 1)


def prepare(links, weights, merged, count, blocks, out):
    def step(t, _):
        cols = pl.ds(pl.multiple_of(t * LANES, LANES), LANES)
        tiles = [tile(links, weights, merged.at[0], cols, blocks)]
        out[0][:, cols] = spread(tiles, 0, 0, blocks)
        out[1][:, cols] = spread(tiles, 1, 0, blocks)
        return 0

    lax.fori_loop(0, count // LANES, step, 0)


def picked(source, start, blocks, index, out):
    lane = jnp.broadcast_to(index & (LANES - 1), (SUB, LANES))
    block = jnp.broadcast_to(index >> 7, (SUB, LANES))
    for r in range(source.shape[0] // SUB):
        rows = slice(r * SUB, (r + 1) * SUB)
        got = None
        for b in range(blocks):
            cols = slice(start + b * LANES, start + (b + 1) * LANES)
            t = jnp.take_along_axis(source[rows, cols], lane, axis=1)
            got = t if got is None else jnp.where(block == b, t, got)
        out[rows, :] = got


def put(ext, padded, at, value):
    high, low = halves(value)
    width = value.shape[1]
    ext[0:padded, at : at + width] = high
    ext[padded : 2 * padded, at : at + width] = low


def product(ext, padded, start, w_high, w_low, cols):
    k = slice(start, start + w_high.shape[0])
    both = jnp.dot(ext[:, k], w_high[:, cols], preferred_element_type=jnp.float32)
    rest = jnp.dot(ext[0:padded, k], w_low[:, cols], preferred_element_type=jnp.float32)
    return both[0:padded] + both[padded : 2 * padded] + rest


def reach(value, links, weights, keep):
    padded = value.shape[0]
    rows = [value[r * SUB : (r + 1) * SUB, :] for r in range(padded // SUB)]
    totals = [None] * len(rows)
    for k in range(links.shape[0]):
        link = jnp.broadcast_to(links[k : k + 1, :], (SUB, LANES))
        weight = jnp.broadcast_to(weights[k : k + 1, :], (SUB, LANES))
        weight = jnp.where(keep(link), weight, 0.0)
        lane = link & (LANES - 1)
        for r, row in enumerate(rows):
            term = weight * jnp.take_along_axis(row, lane, axis=1)
            totals[r] = term if totals[r] is None else totals[r] + term
    return jnp.concatenate(totals, axis=0)


def body(n_patch, n_lev, levels, *refs):
    given, gathered, held, rest = refs[:13], refs[13], refs[14:27], refs[27:]
    field, sc1, sd1, sc2, sd2, pl1, pw1, ul1, uw1, pl2, pw2, ul2, uw2 = held
    (
        xs, ext, ext2, merged, t1h, t1l, w1h, w1l, w3h, w3l, w4h, w4l, p2h, p2l, w2h, w2l, qh, ql,
        det1, sm1, det2, sm2,
        asend, arecv, afar, bsend, brecv, csend, crecv, cfar,
        link1, weight1, link2, weight2, link3, weight3, link4, weight4, rlink1, rweight1, rlink2, rweight2,
        fpart, own2, early1, hsend, hrecv,
        in_sem, x_send, x_recv, m_send, m_recv, g_send, g_recv, h_send, h_recv,
    ) = rest
    tracers, own, cells = field.shape
    rows = own * tracers
    padded = xs.shape[0]
    n1 = cells // 2
    n2 = cells // 4
    halo1 = sc1.shape[2]
    halo2 = sc2.shape[2]
    chunk = cells // n_lev
    b1 = n1 // LANES
    b2 = n2 // LANES
    e1 = n1 + 2 * halo1
    e2 = n2 + 2 * halo2
    wide = 256
    me = lax.axis_index("lev")
    patch = lax.axis_index("patch")

    def away(steps):
        return lax.rem(patch + n_patch + steps, n_patch)

    barrier = pltpu.get_barrier_semaphore()
    for steps in (-2, -1, 1, 2):
        pl.semaphore_signal(barrier, inc=1, device_id={"patch": away(steps)}, device_id_type=MESH)
    for d in range(1, n_lev):
        pl.semaphore_signal(
            barrier, inc=1, device_id={"lev": lax.rem(me + d, n_lev)}, device_id_type=MESH
        )

    coarse = (slice(None), slice(None), slice(n1, cells))
    fine = (slice(None), slice(None), slice(0, n1))
    loads = {0: pltpu.make_async_copy(given[0].at[coarse], field.at[coarse], in_sem.at[0])}
    for i in (1, 5, 6, 2):
        loads[i] = pltpu.make_async_copy(given[i], held[i], in_sem.at[i])
    loads[13] = pltpu.make_async_copy(given[0].at[fine], field.at[fine], in_sem.at[13])
    for i in (3, 4, 7, 8, 9, 10, 11, 12):
        loads[i] = pltpu.make_async_copy(given[i], held[i], in_sem.at[i])
    for load in loads.values():
        load.start()

    def loaded(*which):
        for i in which:
            loads[i].wait()

    def pack(start, stop):
        if padded > rows:
            edge = rows // SUB * SUB
            xs[edge:padded, start:stop] = jnp.zeros((padded - edge, stop - start), jnp.float32)
        for t in range(tracers):
            xs[t * own : (t + 1) * own, start:stop] = field[t, :, start:stop]

    def message(which, side, steps, source, target):
        return pltpu.make_async_remote_copy(
            src_ref=source.at[side],
            dst_ref=target.at[side],
            send_sem=x_send.at[which, side],
            recv_sem=x_recv.at[which, side],
            device_id={"patch": away(-steps if side else steps)},
            device_id_type=MESH,
        )

    near1 = [message(0, side, 1, asend, arecv) for side in range(2)]
    far1 = [message(1, side, 2, asend, afar) for side in range(2)]
    part1 = [message(2, side, 1, bsend, brecv) for side in range(2)]
    near2 = [message(3, side, 1, csend, crecv) for side in range(2)]
    far2 = [message(4, side, 2, csend, cfar) for side in range(2)]

    def meta(which, side, source, target):
        return pltpu.make_async_remote_copy(
            src_ref=source,
            dst_ref=target.at[side],
            send_sem=m_send.at[which, side],
            recv_sem=m_recv.at[which, side],
            device_id={"patch": away(-1 if side else 1)},
            device_id_type=MESH,
        )

    def half(ref, side):
        return ref.at[:, side * LANES : (side + 1) * LANES]

    meta1 = [meta(0, side, half(link1, side), rlink1) for side in range(2)]
    meta1 += [meta(1, side, half(weight1, side), rweight1) for side in range(2)]
    meta2 = [meta(2, side, link2, rlink2) for side in range(2)]
    meta2 += [meta(3, side, weight2, rweight2) for side in range(2)]

    outgoing = []

    def scatter(source, base):
        for piece in range(source.shape[1] // chunk):
            d = base // chunk + piece
            part = source.at[:, piece * chunk : (piece + 1) * chunk]
            copy = pltpu.make_async_remote_copy(
                src_ref=part,
                dst_ref=gathered.at[me],
                send_sem=g_send.at[d],
                recv_sem=g_recv.at[me],
                device_id={"lev": d},
                device_id_type=MESH,
            )
            outgoing.append((d, copy))

            @pl.when(me != d)
            def _():
                copy.start()

            @pl.when(me == d)
            def _():
                gathered[d] = part[...]

    lower = lax.broadcasted_iota(jnp.int32, (padded, LANES), 1) < halo2
    first = lax.broadcasted_iota(jnp.int32, (SUB, LANES), 1) < halo2

    def two(send):
        return jnp.concatenate([send[0, 1:2, :], send[0, 0:1, :]], axis=1)

    def side1(side):
        start = n1 + side * halo1
        return lambda link: (link >= start) & (link < start + halo1)

    def side2(same):
        def keep(link):
            ours = (link < n2 + halo2) == first
            return (link >= n2) & (ours if same else ~ours)

        return keep

    loaded(0, 1)
    pack(n1, cells)
    for side in range(2):
        picked(xs, n1, b1, sc1[0, 1 - side : 2 - side, :], asend.at[side])
    put(ext, padded, 0, xs[:, n1:cells])
    loaded(2, 5, 6, 13, 3, 4, 7, 8, 9, 10, 11, 12)
    pack(0, n1)

    def fine1(cols, got):
        det1[:, cols] = xs[:, cols] - got

    def detail():
        stage(pl1, pw1, merged, 0, n1, b1, e1 // LANES, ext, (t1h, t1l), fine1)

    def level2():
        prepare(link2, weight2, merged, LANES, b2, (w4h, w4l))
        prepare(pl2, pw2, merged, n2, e2 // LANES, (p2h, p2l))
        prepare(ul2, uw2, merged, n2, e2 // LANES, (w2h, w2l))

    for side in range(2):
        index = sd1[0, 1 - side : 2 - side, :]
        picked(pl1, 0, b1, index, half(link1, side))
        picked(pw1, 0, b1, index, half(weight1, side))
    picked(pl2, 0, b2, two(sd2), link2)
    picked(pw2, 0, b2, two(sd2), weight2)
    picked(ul1, 0, b2, two(sd2), link4)
    picked(uw1, 0, b2, two(sd2), weight4)

    @pl.when(patch < 2)
    def _():
        detail()
        level2()

    pl.semaphore_wait(barrier, 4 + n_lev - 1)
    for copy in near1 + far1 + meta1 + meta2:
        copy.start()

    @pl.when(patch >= 2)
    def _():
        detail()

    for side in range(2):
        picked(det1, 0, b1, sd1[0, 1 - side : 2 - side, :], bsend.at[side])
    for copy in part1:
        copy.start()
    picked(xs, n1, b2, two(sd2), fpart.at[0])
    prepare(ul1, uw1, merged, n1, e1 // LANES, (w1h, w1l))
    prepare(link4, weight4, merged, LANES, e1 // LANES, (w3h, w3l))

    @pl.when(patch >= 2)
    def _():
        level2()

    for side in range(2):
        near1[side].wait_recv()
        put(ext, padded, n1 + side * halo1, arecv[side])
    for c in range(0, n1, wide):
        cols = slice(c, c + wide)
        det1[:, cols] = det1[:, cols] - product(ext, padded, n1, t1h, t1l, cols)
    scatter(det1, 0)
    put(ext, padded, 0, det1[...])
    for copy in meta1 + far1:
        copy.wait_recv()
    for side in range(2):
        known = reach(asend[1 - side], rlink1.at[side], rweight1.at[side], side1(1 - side))
        outer = reach(afar[side], rlink1.at[side], rweight1.at[side], side1(side))
        early1[side] = known + outer
    for side in range(2):
        part1[side].wait_recv()
        put(ext, padded, n1 + side * halo1, brecv[side] - early1[side])

    def smooth(start, stop):
        for c in range(start, stop, wide):
            cols = slice(c, c + wide)
            sm1[:, cols] = xs[:, n1 + c : n1 + c + wide] + product(ext, padded, 0, w1h, w1l, cols)

    smooth(n2, n1)
    put(ext2, padded, 0, sm1[:, n2:n1])
    picked(sm1, n2, b2, two(sc2), own2)
    every_lane = slice(0, LANES)
    part = fpart[0] + product(ext, padded, 0, w3h, w3l, every_lane)
    part = part - product(ext2, padded, 0, w4h, w4l, every_lane)
    part = pltpu.roll(part, halo2, axis=1)
    csend[0] = jnp.where(lower, own2[...], part)
    csend[1] = jnp.where(lower, part, own2[...])
    for copy in near2 + far2:
        copy.start()

    smooth(0, n2)
    own_rows = slice(0, n2)
    for c in range(0, n2, wide):
        cols = slice(c, c + wide)
        got = product(ext2, padded, 0, p2h.at[own_rows], p2l.at[own_rows], cols)
        det2[:, cols] = sm1[:, cols] - got
    scatter(det2, n1)
    put(ext2, padded, 0, det2[...])
    for copy in meta2:
        copy.wait_recv()
    turned = lax.broadcasted_iota(jnp.int32, (rlink2.shape[1], LANES), 1) < halo2
    link3[...] = jnp.where(turned, rlink2[0], rlink2[1])
    weight3[...] = jnp.where(turned, rweight2[0], rweight2[1])
    put(ext2, padded, n2, -reach(own2[...], link3, weight3, side2(False)))

    for c in range(0, n2, wide):
        cols = slice(c, c + wide)
        sm2[:, cols] = sm1[:, n2 + c : n2 + c + wide] + product(ext2, padded, 0, w2h, w2l, cols)
    scatter(sm2, n1 + n2)

    @pl.when(me >= (n1 + n2) // chunk)
    def _():
        for c in range(0, n2, wide):
            cols = slice(c, c + wide)
            both = jnp.concatenate([p2h[n2:e2, :], p2l[n2:e2, :]], axis=0)
            both = jnp.dot(both, w2h[own_rows, cols], preferred_element_type=jnp.float32)
            rest = jnp.dot(p2h[n2:e2, :], w2l[own_rows, cols], preferred_element_type=jnp.float32)
            high, low = halves(-(both[0:LANES] + both[LANES : 2 * LANES] + rest))
            qh[0:LANES, cols] = high
            ql[0:LANES, cols] = low
            qh[LANES : 2 * LANES, cols] = w2h[n2:e2, cols]
            ql[LANES : 2 * LANES, cols] = w2l[n2:e2, cols]

    for copy in near2 + far2:
        copy.wait_recv()
    hsend[0] = jnp.where(lower, crecv[0], crecv[1])
    value = pltpu.roll(jnp.where(lower, crecv[1], crecv[0]), halo2, axis=1)
    outer = jnp.where(lower, cfar[0], cfar[1])
    hsend[1] = value - reach(outer, link3, weight3, side2(True))

    forward = []
    for piece in range(2 * n2 // chunk):
        d = n1 // chunk + piece
        count = 1 if piece < n2 // chunk else 2
        copy = pltpu.make_async_remote_copy(
            src_ref=hsend.at[0:count],
            dst_ref=hrecv.at[me, 0:count],
            send_sem=h_send.at[piece],
            recv_sem=h_recv.at[me],
            device_id={"lev": d},
            device_id_type=MESH,
        )
        forward.append((d, copy))

        @pl.when(me != d)
        def _():
            copy.start()

        @pl.when(me == d)
        def _():
            hrecv[d, 0:count] = hsend[0:count]

    for s in range(n_lev):

        @pl.when(me != s)
        def _():
            pltpu.make_async_remote_copy(
                src_ref=gathered.at[s],
                dst_ref=gathered.at[s],
                send_sem=g_send.at[s],
                recv_sem=g_recv.at[s],
                device_id={"lev": s},
                device_id_type=MESH,
            ).wait_recv()

    def arrived(count):
        for s in range(n_lev):

            @pl.when(me != s)
            def _():
                pltpu.make_async_remote_copy(
                    src_ref=hrecv.at[s, 0:count],
                    dst_ref=hrecv.at[s, 0:count],
                    send_sem=h_send.at[0],
                    recv_sem=h_recv.at[s],
                    device_id={"lev": s},
                    device_id_type=MESH,
                ).wait_recv()

    def times(value, high, low):
        top, rest = halves(value)
        count = value.shape[0]
        both = jnp.concatenate([top, rest], axis=0)
        both = jnp.dot(both, high, preferred_element_type=jnp.float32)
        rest = jnp.dot(top, low, preferred_element_type=jnp.float32)
        return both[0:count] + both[count : 2 * count] + rest

    def every(which):
        return jnp.concatenate([hrecv[s, which] for s in range(n_lev)], axis=0)

    @pl.when((me >= n1 // chunk) & (me < (n1 + n2) // chunk))
    def _():
        arrived(1)
        cols = pl.ds(pl.multiple_of((me - n1 // chunk) * chunk, LANES), chunk)
        change = times(every(0), p2h[n2:e2, cols], p2l[n2:e2, cols])
        for s in range(n_lev):
            gathered[s] = gathered[s] - change[s * padded : (s + 1) * padded]

    @pl.when(me >= (n1 + n2) // chunk)
    def _():
        arrived(2)
        cols = pl.ds(pl.multiple_of((me - (n1 + n2) // chunk) * chunk, LANES), chunk)
        change = times(jnp.concatenate([every(0), every(1)], axis=1), qh[:, cols], ql[:, cols])
        for s in range(n_lev):
            gathered[s] = gathered[s] + change[s * padded : (s + 1) * padded]

    for group in (near1, far1, part1, near2, far2, meta1, meta2):
        for copy in group:
            copy.wait_send()
    for d, copy in outgoing + forward:

        @pl.when(me != d)
        def _():
            copy.wait_send()


def transform(gathered, t_high, t_low, out, staged, sems):
    groups, padded, chunk = gathered.shape
    tracers, levels, _ = out.shape
    high, low = halves(gathered[...].reshape(groups * padded, chunk))
    copies = []
    for t in range(tracers):
        rows = slice(t * levels, (t + 1) * levels)
        staged[t] = (
            jnp.dot(t_high[rows, :], high, preferred_element_type=jnp.float32)
            + jnp.dot(t_high[rows, :], low, preferred_element_type=jnp.float32)
            + jnp.dot(t_low[rows, :], high, preferred_element_type=jnp.float32)
        )
        copies.append(pltpu.make_async_copy(staged.at[t], out.at[t], sems.at[t]))
        copies[t].start()
    for copy in copies:
        copy.wait()


def on_device(n_patch, n_lev, *args):
    field, sc1 = args[0], args[1]
    own, tracers, cells = field.shape
    levels = own * n_lev
    rows = own * tracers
    padded = -(-rows // (2 * SUB)) * (2 * SUB)
    n1, n2 = cells // 2, cells // 4
    e1 = n1 + 2 * sc1.shape[2]
    e2 = n2 + 2 * args[3].shape[2]
    chunk = cells // n_lev
    slots = args[5].shape[0]
    t_high, t_low = spread_table(levels, tracers, n_lev, padded)
    f32, bf16 = jnp.float32, jnp.bfloat16
    gathered = pl.pallas_call(
        functools.partial(body, n_patch, n_lev, levels),
        out_shape=jax.ShapeDtypeStruct((n_lev, padded, chunk), f32),
        in_specs=[pl.BlockSpec(memory_space=pltpu.HBM)] * 13,
        out_specs=pl.BlockSpec(memory_space=pltpu.VMEM),
        scratch_shapes=[
            pltpu.VMEM((tracers, own, cells), f32),
            *(pltpu.VMEM(a.shape, a.dtype) for a in args[1:]),
            pltpu.VMEM((padded, cells), f32),
            pltpu.VMEM((2 * padded, e1), bf16),
            pltpu.VMEM((2 * padded, e2), bf16),
            pltpu.VMEM((2, slots * -(-(e1 // LANES) // SUB) * SUB, LANES), f32),
            *[pltpu.VMEM((e1 - n1, n1), bf16)] * 2,
            *[pltpu.VMEM((e1, n1), bf16)] * 2,
            *[pltpu.VMEM((e1, LANES), bf16)] * 2,
            *[pltpu.VMEM((n2, LANES), bf16)] * 2,
            *[pltpu.VMEM((e2, n2), bf16)] * 4,
            *[pltpu.VMEM((2 * (e2 - n2), n2), bf16)] * 2,
            *[pltpu.VMEM((padded, n1), f32)] * 2,
            *[pltpu.VMEM((padded, n2), f32)] * 2,
            *[pltpu.VMEM((2, padded, LANES), f32)] * 8,
            pltpu.VMEM((slots, 2 * LANES), jnp.int32),
            pltpu.VMEM((slots, 2 * LANES), f32),
            pltpu.VMEM((slots, LANES), jnp.int32),
            pltpu.VMEM((slots, LANES), f32),
            pltpu.VMEM((slots, LANES), jnp.int32),
            pltpu.VMEM((slots, LANES), f32),
            pltpu.VMEM((slots, LANES), jnp.int32),
            pltpu.VMEM((slots, LANES), f32),
            pltpu.VMEM((2, slots, LANES), jnp.int32),
            pltpu.VMEM((2, slots, LANES), f32),
            pltpu.VMEM((2, slots, LANES), jnp.int32),
            pltpu.VMEM((2, slots, LANES), f32),
            pltpu.VMEM((2, padded, LANES), f32),
            pltpu.VMEM((padded, LANES), f32),
            pltpu.VMEM((2, padded, LANES), f32),
            pltpu.VMEM((2, padded, LANES), f32),
            pltpu.VMEM((n_lev, 2, padded, LANES), f32),
            pltpu.SemaphoreType.DMA((14,)),
            pltpu.SemaphoreType.DMA((5, 2)),
            pltpu.SemaphoreType.DMA((5, 2)),
            pltpu.SemaphoreType.DMA((4, 2)),
            pltpu.SemaphoreType.DMA((4, 2)),
            pltpu.SemaphoreType.DMA((n_lev,)),
            pltpu.SemaphoreType.DMA((n_lev,)),
            pltpu.SemaphoreType.DMA((2 * n2 // chunk,)),
            pltpu.SemaphoreType.DMA((n_lev,)),
        ],
        compiler_params=pltpu.CompilerParams(
            collective_id=0, has_side_effects=True, vmem_limit_bytes=24 << 20
        ),
    )(*(pltpu.with_memory_space_constraint(a, pltpu.HBM) for a in (jnp.transpose(field, (1, 0, 2)), *args[1:])))
    result = pl.pallas_call(
        transform,
        out_shape=jax.ShapeDtypeStruct((tracers, levels, chunk), f32),
        in_specs=[pl.BlockSpec(memory_space=pltpu.VMEM)] * 3,
        out_specs=pl.BlockSpec(memory_space=pltpu.HBM),
        scratch_shapes=[
            pltpu.VMEM((tracers, levels, chunk), f32),
            pltpu.SemaphoreType.DMA((tracers,)),
        ],
        compiler_params=pltpu.CompilerParams(vmem_limit_bytes=8 << 20),
    )(gathered, jnp.asarray(t_high), jnp.asarray(t_low))
    return jnp.transpose(result, (1, 0, 2))


def solution(mesh):
    in_specs = (P("lev", None, "patch"),)
    in_specs += (P("patch", None, None),) * 4
    in_specs += (P(None, "patch"),) * 8
    out_specs = P(None, None, ("patch", "lev"))
    fn = functools.partial(on_device, mesh.shape["patch"], mesh.shape["lev"])
    return jax.shard_map(
        fn, mesh=mesh, in_specs=in_specs, out_specs=out_specs, check_vma=False
    )
```
